512 devices in a mesh: tm: 32 (over x, z), frame: 16 (over y, core).
Axes of the slice: x: 4, y: 8, z: 8, core: 2. Of those that a mesh axis runs over, the one named last changes fastest.
Arguments:
- start_state: float32 [16, 32, 32, 128], P('frame'), may hold values from -6 to 6
- initial_guess: float32 [32, 16, 32, 32, 128], P('tm', 'frame'), may hold values from -6 to 6
- noise_draws: float32 [32, 16, 32, 32, 128], P('tm', 'frame'), may hold values from -6 to 6
- timesteps: int32 [32], P('tm'), may hold values from 0 to 999
- gain_space: float32 [128], replicated, may hold values from 0.1 to 1.9
- gain_attention: float32 [128], replicated, may hold values from 0.1 to 1.9
- time_weight: float32 [128, 256], replicated, may hold values from -0.5 to 0.5
- space_weight: bfloat16 [1152, 128], replicated, may hold values from -0.1875 to 0.1875
- attention_weight: bfloat16 [128, 384], replicated, may hold values from -4 to 4
- output_weight: bfloat16 [128, 128], replicated, may hold values from -0.5 to 0.5
Outputs:
- advanced: float32 [32, 16, 32, 32, 128], P('tm', 'frame')
The draws below stay inside these ranges and needn't reach their ends.
All inputs are finite; a program needn't handle non-finite values.
Results may differ from the reference program's by a relative error of at most 0.0025.
Values may be sent and summed in bfloat16 or wider, within the bound.
No kernel may reach another device: no remote copies, remote signals or barrier semaphores. Data moves between devices by JAX's collectives and lax.ppermute only.
A program may use at most 64 MiB of HBM per device.

```python
import math
import jax
import jax.numpy as jnp
from jax import lax

C = 128
HEAD_DIM = 64
H = 32
W = 32
ITERS = 2
FRAMES = 16
STEPS = 32


def draw_attention_weight(key, part):
    drawn = jax.random.normal(jax.random.fold_in(key, 7), (C, 3 * C), jnp.float32) / math.sqrt(C)
    return jnp.clip(drawn, -4.0, 4.0).astype(jnp.bfloat16)


def touch_ends(values, stream_key, least, high):
    extent = values.shape
    index_at = [jax.random.randint(jax.random.fold_in(stream_key, axis), (), 0, extent[axis]) for axis in range(len(extent))]
    values = values.at[tuple(index_at)].set(least)
    longest = extent.index(max(extent))
    index_at[longest] = (index_at[longest] + 1) % extent[longest]
    return values.at[tuple(index_at)].set(high)


def shard_levels(own_key, extent, split, smallest, top_value):
    def one(position, parts):
        heights = jax.random.uniform(jax.random.fold_in(jax.random.fold_in(own_key, 6), position), (parts,), jnp.float32, smallest / len(split), top_value / len(split))
        return jnp.repeat(jnp.exp(heights), extent[position] // parts).reshape((-1,) + (1,) * (len(extent) - position - 1))

    level = one(*split[0])
    for cut in split[1:]:
        level = level * one(*cut)
    return level


def noise(key, extent, width, reach, pieces=(), kind=jnp.bfloat16):
    array = width * jax.random.normal(key, extent, jnp.float32)
    if pieces:
        array = array * shard_levels(key, extent, pieces, -0.22, 0.18)
    return jnp.clip(array, -reach, reach).astype(kind)


def setup_inputs(seed: int = 0) -> dict:
    keys = jax.random.split(jax.random.key(seed), 11)
    start_state = noise(keys[0], (FRAMES, H, W, C), 1.0, 6.0, ((0, 16),), jnp.float32)
    initial_guess = noise(keys[1], (STEPS, FRAMES, H, W, C), 1.0, 6.0, ((0, 32), (1, 16)), jnp.float32)
    noise_draws = noise(keys[2], (STEPS, FRAMES, H, W, C), 1.0, 6.0, ((0, 32), (1, 16)), jnp.float32)
    timesteps = touch_ends(jax.random.randint(keys[3], (STEPS,), 0, 1000), jax.random.fold_in(keys[3], 1), 0, 999).astype(jnp.int32)
    gain_space = jnp.clip(1.0 + 0.18 * jax.random.normal(keys[4], (C,), jnp.float32), 0.1, 1.9)
    gain_attention = jnp.clip(1.0 + 0.18 * jax.random.normal(keys[5], (C,), jnp.float32), 0.1, 1.9)
    time_weight = noise(keys[6], (C, 2 * C), C ** -0.5, 0.5, (), jnp.float32)
    space_weight = noise(keys[7], (9 * C, C), (9 * C) ** -0.5, 0.1875)
    attention_weight = draw_attention_weight(jax.random.fold_in(keys[10], 71), 0)
    output_weight = noise(keys[9], (C, C), C ** -0.5, 0.5)
    return {"start_state": start_state, "initial_guess": initial_guess, "noise_draws": noise_draws, "timesteps": timesteps, "gain_space": gain_space, "gain_attention": gain_attention, "time_weight": time_weight, "space_weight": space_weight, "attention_weight": attention_weight, "output_weight": output_weight}


def embed_time(step_value):
    half_width = C // 2
    frequency = jnp.exp(-math.log(10000.0) * jnp.arange(half_width, dtype=jnp.float32) / half_width)
    angles = step_value.astype(jnp.float32) * frequency
    return jnp.concatenate([jnp.cos(angles), jnp.sin(angles)])

def modulation(step_value, time_weight):
    encoded = embed_time(step_value)[None, :]
    shifted = jnp.dot(encoded, time_weight, precision=lax.Precision.HIGHEST, preferred_element_type=jnp.float32)[0]
    return (1.0 + shifted[:C], shifted[C:])

def normalize(field, gain):
    return field * lax.rsqrt(lax.optimization_barrier(jnp.mean(field * field, axis=-1, keepdims=True)) + 1e-06) * gain

def conv_taps(padded, space_weight):
    frames_here = padded.shape[0]
    rows_here = padded.shape[1] - 2
    cols_here = padded.shape[2] - 2
    shifted = [padded[:, row_shift:row_shift + rows_here, col_shift:col_shift + cols_here, :] for row_shift in range(3) for col_shift in range(3)]
    stacked = jnp.concatenate(shifted, axis=-1).reshape(-1, 9 * padded.shape[3])
    result = jnp.dot(stacked, space_weight, preferred_element_type=jnp.float32)
    return result.reshape(frames_here, rows_here, cols_here, space_weight.shape[1])

def attend(normed_in, attention_weight):
    frames_all, rows_here, cols_here, channels = normed_in.shape
    projected = jnp.dot(normed_in.reshape(-1, channels), attention_weight, preferred_element_type=jnp.float32).astype(jnp.bfloat16)
    projected = lax.optimization_barrier(projected).astype(jnp.float32)
    projected = projected.reshape(frames_all, rows_here, cols_here, 3, channels // HEAD_DIM, HEAD_DIM)
    query_vectors = projected[:, :, :, 0]
    key_vectors = projected[:, :, :, 1]
    value_vectors = projected[:, :, :, 2]
    scores = jnp.einsum('fxyhd,gxyhd->xyhfg', query_vectors, key_vectors) / math.sqrt(HEAD_DIM)
    weights = jax.nn.softmax(scores, axis=-1).astype(jnp.bfloat16)
    weights = lax.optimization_barrier(weights).astype(jnp.float32)
    attended = jnp.einsum('xyhfg,gxyhd->fxyhd', weights, value_vectors)
    return attended.reshape(frames_all, rows_here, cols_here, channels).astype(jnp.bfloat16)

def drift(state, step_value, gain_space, gain_attention, time_weight, space_weight, attention_weight, output_weight):
    scaling, offset = modulation(step_value, time_weight)
    normed = (normalize(state, gain_space) * scaling + offset).astype(jnp.bfloat16)
    padded = jnp.pad(normed, ((0, 0), (1, 1), (1, 1), (0, 0)))
    mixed_state = state + jax.nn.silu(conv_taps(padded, space_weight))
    attn_in = normalize(mixed_state, gain_attention).astype(jnp.bfloat16)
    attended = attend(attn_in, attention_weight)
    projected = jnp.dot(attended.reshape(-1, attended.shape[-1]), output_weight, preferred_element_type=jnp.float32)
    return mixed_state + projected.reshape(mixed_state.shape)

def reference(start_state, initial_guess, noise_draws, timesteps, gain_space, gain_attention, time_weight, space_weight, attention_weight, output_weight):
    steps_total = timesteps.shape[0]
    time_values = timesteps.astype(jnp.float32) / 1000.0
    coefficient = (0.5 + time_values) / math.sqrt(steps_total)

    def one_term(carried):
        state, noise_block, step_value, time_value, coeff_value = carried
        evaluated = drift(state, step_value, gain_space, gain_attention, time_weight, space_weight, attention_weight, output_weight)
        return coeff_value * (evaluated + time_value * noise_block)
    iterate = initial_guess
    before = jnp.zeros_like(initial_guess)
    terms = jnp.zeros_like(initial_guess)
    for picard_turn in range(ITERS):
        terms = lax.map(one_term, (iterate, noise_draws, timesteps, time_values, coefficient))
        before = jnp.cumsum(terms, axis=0) - terms
        iterate = start_state[None] + before
    return start_state[None] + (before + terms)
```

```python
import math

import jax
import jax.numpy as jnp
from jax import lax
from jax.experimental import pallas as pl
from jax.experimental.pallas import tpu as pltpu
from jax.sharding import Mesh
from jax.sharding import PartitionSpec as P

C = 128
HEAD_DIM = 64
FRAMES = 16
STEPS = 32
SIDE = 32
CELLS = SIDE * SIDE
TM = ("tm_0", "tm_1")
ALL = ("tm_0", "tm_1", "frame")
F32 = jnp.float32
BF16 = jnp.bfloat16
VMEM = pl.BlockSpec(memory_space=pltpu.VMEM)
SMEM = pl.BlockSpec(memory_space=pltpu.SMEM)


def dot(left, right):
    return jnp.dot(left, right, preferred_element_type=F32)


def unit(field, gain):
    return field * lax.rsqrt(jnp.mean(field * field, axis=-1, keepdims=True) + 1e-06) * gain


def attention_masks():
    row = lax.broadcasted_iota(jnp.int32, (128, 128), 0)
    lane = lax.broadcasted_iota(jnp.int32, (128, 128), 1)
    return row // FRAMES == lane // FRAMES, lane < HEAD_DIM


def attend_block(mixed, gain, attention_weight, output_weight, masks):
    same_cell, first_head = masks
    projected = dot(unit(mixed, gain).astype(BF16), attention_weight).astype(BF16)
    queries, keys, values = (projected[:, i * C : (i + 1) * C] for i in range(3))
    zero = jnp.zeros((), BF16)
    attended = None
    for head in range(2):
        lanes = first_head if head == 0 else jnp.logical_not(first_head)
        scores = lax.dot_general(
            jnp.where(lanes, queries, zero), keys, (((1,), (1,)), ((), ())), preferred_element_type=F32
        ) * (1.0 / math.sqrt(HEAD_DIM))
        scores = jnp.where(same_cell, scores, -1e30)
        grown = jnp.exp(scores - jnp.max(scores, axis=-1, keepdims=True))
        weights = (grown * (1.0 / jnp.sum(grown, axis=-1, keepdims=True))).astype(BF16)
        part = dot(weights, jnp.where(lanes, values, zero))
        attended = part if attended is None else attended + part
    return dot(attended.astype(BF16), output_weight)


def first_kernel(
    scalars, guess, noise, start, gain, scaling, offset, space_weight, out, padded, plain, packed
):
    col = lax.broadcasted_iota(jnp.int32, (8, SIDE, C), 1)
    padded[0] = jnp.zeros((SIDE, 3 * C), BF16)
    padded[SIDE + 1] = jnp.zeros((SIDE, 3 * C), BF16)
    for block in range(4):
        rows = pl.ds(block * 8, 8)
        state = guess[rows]
        normed = unit(state, gain[...]) * scaling[...] + offset[...]
        left = jnp.where(col == 0, 0.0, pltpu.roll(normed, 1, 1))
        right = jnp.where(col == SIDE - 1, 0.0, pltpu.roll(normed, SIDE - 1, 1))
        at = pl.ds(block * 8 + 1, 8)
        padded[at, :, 0:C] = left.astype(BF16)
        padded[at, :, C : 2 * C] = normed.astype(BF16)
        padded[at, :, 2 * C : 3 * C] = right.astype(BF16)
    total = None
    for shift in range(3):
        part = dot(
            padded[shift : shift + SIDE].reshape(CELLS, 3 * C),
            space_weight[shift * 3 * C : (shift + 1) * 3 * C, :],
        )
        total = part if total is None else total + part
    plain[...] = total
    scale = scalars[0]
    last = scalars[1] > 0.5
    for block in range(8):
        rows = pl.ds(block * 128, 128)
        conv = plain[rows, :]
        mixed = guess[pl.ds(block * 4, 4)].reshape(128, C) + conv * jax.nn.sigmoid(conv)
        begun = start[pl.ds(block * 4, 4)].reshape(128, C)
        begun_high = begun.astype(BF16).astype(F32)
        plain[rows, :] = jnp.where(last, begun - begun_high, mixed)
        drawn = noise[pl.ds(block * 4, 4)].reshape(128, C) * scale
        packed[pl.ds(CELLS + block * 128, 128), :] = jnp.where(last, begun_high, drawn)
    for block in range(8):
        half = CELLS // 16
        for slot in range(4):
            if slot < 2:
                piece = plain[pl.ds(block * 128 + slot, half, 2), :]
            else:
                piece = packed[pl.ds(CELLS + block * 128 + slot - 2, half, 2), :]
            packed[pl.ds(2 * CELLS + slot, half, 4), :] = piece
        out[pl.ds(block * 256, 256), :] = packed[pl.ds(2 * CELLS, 256), :].astype(BF16)


def owner_kernel(coefficients, received, gain, attention_weight, output_weight, states, noise_before, wide, drifts):
    masks = attention_masks()
    wide[...] = received[...].astype(F32)
    for cell in range(2):
        for block in range(4):
            mixed = wide[pl.ds(block * 512 + cell, 128, 4), :]
            drifts[pl.ds(cell * 512 + block * 128, 128), :] = mixed + attend_block(
                mixed, gain[...], attention_weight[...], output_weight[...], masks
            )
    for cell in range(2):
        tail = (STEPS - 1) * FRAMES * 4 + cell
        state = wide[pl.ds(tail + 2, FRAMES, 4), :] + wide[pl.ds(tail, FRAMES, 4), :]
        noises = jnp.zeros((FRAMES, C), F32)
        for step in range(STEPS):
            rows = pl.ds(step * 32 + cell * FRAMES, FRAMES)
            states[rows, :] = state.astype(BF16)
            noise_before[rows, :] = noises
            if step < STEPS - 1:
                drawn = wide[pl.ds(step * FRAMES * 4 + 2 + cell, FRAMES, 4), :]
                drift = drifts[pl.ds(cell * 512 + step * FRAMES, FRAMES), :]
                state = state + (coefficients[step] * drift + drawn)
                noises = noises + drawn


def norm_kernel(state, gain, scaling, offset, first, second):
    for cell, out in ((0, first), (1, second)):
        for block in range(4):
            rows = state[pl.ds(block * 8, 8), cell].astype(F32)
            normed = unit(rows, gain[...]) * scaling[...] + offset[...]
            out[pl.ds(block * 8, 8)] = normed.astype(BF16)


def second_kernel(
    scalars, state, left, first, second, right, space_weight, gain, attention_weight, output_weight, out, padded, conv
):
    for col, piece in enumerate((left, first, second, right)):
        padded[col, 0] = jnp.zeros((FRAMES, C), BF16)
        padded[col, SIDE + 1] = jnp.zeros((FRAMES, C), BF16)
        padded[col, 1 : SIDE + 1] = piece[...]
    for cell in range(2):
        taps = [
            padded[cell + across, down : down + SIDE].reshape(SIDE * FRAMES, C)
            for down in range(3)
            for across in range(3)
        ]
        conv[cell] = dot(jnp.concatenate(taps, axis=-1), space_weight[...])
    masks = attention_masks()
    coefficient = scalars[2]
    for cell in range(2):
        for block in range(4):
            found = conv[cell, pl.ds(block * 128, 128), :]
            here = state[pl.ds(block * 8, 8), cell].reshape(128, C).astype(F32)
            mixed = here + found * jax.nn.sigmoid(found)
            drift = mixed + attend_block(
                mixed, gain[...], attention_weight[...], output_weight[...], masks
            )
            out[pl.ds(block * 8, 8), cell] = (coefficient * drift).reshape(8, FRAMES, C).astype(BF16)


def sum_kernel(received, noise_before, out):
    for cell in range(2):
        total = jnp.zeros((FRAMES, C), F32)
        for step in range(STEPS):
            rows = pl.ds(step * 32 + cell * FRAMES, FRAMES)
            total = total + received[rows, :].astype(F32)
            out[pl.ds(step * 32 + cell, FRAMES, 2), :] = total + noise_before[rows, :]


def call(kernel, outs, operands, scratch, scalar_first, flops):
    specs = [SMEM if scalar_first and i == 0 else VMEM for i in range(len(operands))]
    moved = sum(x.size * x.dtype.itemsize for x in (*operands, *outs))
    return pl.pallas_call(
        kernel,
        out_shape=outs,
        in_specs=specs,
        out_specs=[VMEM] * len(outs),
        scratch_shapes=scratch,
        cost_estimate=pl.CostEstimate(flops=flops, bytes_accessed=moved, transcendentals=0),
    )(*operands)


def struct(shape, dtype):
    return jax.ShapeDtypeStruct(shape, dtype)


def embed_time(step_value):
    half_width = C // 2
    frequency = jnp.exp(-math.log(10000.0) * jnp.arange(half_width, dtype=F32) / half_width)
    angles = step_value.astype(F32) * frequency
    return jnp.concatenate([jnp.cos(angles), jnp.sin(angles)])


def modulation(step_value, time_weight):
    encoded = embed_time(step_value)[None, :]
    shifted = jnp.dot(encoded, time_weight, precision=lax.Precision.HIGHEST, preferred_element_type=F32)
    return (1.0 + shifted[:, :C], shifted[:, C:])


def exchange(array, axes):
    return lax.all_to_all(array, axes, 0, 0, tiled=True)


def shards(
    start_state,
    initial_guess,
    noise_draws,
    timesteps,
    gain_space,
    gain_attention,
    time_weight,
    space_weight,
    attention_weight,
    output_weight,
):
    steps_total = lax.axis_size(TM)
    step_value = timesteps[0]
    time_value = step_value.astype(F32) / 1000.0
    coefficient = (0.5 + time_value) / math.sqrt(steps_total)
    scaling, offset = modulation(step_value, time_weight)
    guess, noise, start = initial_guess[0, 0], noise_draws[0, 0], start_state[0]
    gain_s, gain_a = gain_space[None, :], gain_attention[None, :]
    is_last = (lax.axis_index(TM) == steps_total - 1).astype(F32)
    scalars = jnp.stack([coefficient * time_value, is_last, coefficient])

    (sent,) = call(
        first_kernel,
        [struct((2 * CELLS, C), BF16)],
        (scalars, guess, noise, start, gain_s, scaling, offset, space_weight),
        [
            pltpu.VMEM((SIDE + 2, SIDE, 3 * C), BF16),
            pltpu.VMEM((CELLS, C), F32),
            pltpu.VMEM((2 * CELLS + 256, C), F32),
        ],
        True,
        2 * CELLS * 9 * C * C,
    )
    received = exchange(sent.reshape(512, 4, C), ALL).reshape(2 * CELLS, C)
    all_steps = lax.all_gather(timesteps, TM, tiled=True)
    coefficients = (0.5 + all_steps.astype(F32) / 1000.0) / math.sqrt(steps_total)
    states, noise_before = call(
        owner_kernel,
        [struct((CELLS, C), BF16), struct((CELLS, C), F32)],
        (coefficients, received, gain_a, attention_weight, output_weight),
        [pltpu.VMEM((2 * CELLS, C), F32), pltpu.VMEM((CELLS, C), F32)],
        True,
        2 * CELLS * 8 * C * C,
    )
    state = exchange(states.reshape(32, 32, C), TM).reshape(SIDE, 2, FRAMES, C)
    first, second = call(
        norm_kernel,
        [struct((SIDE, FRAMES, C), BF16)] * 2,
        (state, gain_s, scaling, offset),
        [],
        False,
        10 * CELLS * C,
    )
    count = lax.axis_size("frame")
    left = lax.ppermute(second, "frame", [(k, k + 1) for k in range(count - 1)])
    right = lax.ppermute(first, "frame", [(k + 1, k) for k in range(count - 1)])
    (drifts,) = call(
        second_kernel,
        [struct((SIDE, 2, FRAMES, C), BF16)],
        (scalars, state, left, first, second, right, space_weight, gain_a, attention_weight, output_weight),
        [pltpu.VMEM((4, SIDE + 2, FRAMES, C), BF16), pltpu.VMEM((2, CELLS // 2, C), F32)],
        True,
        2 * CELLS * 17 * C * C,
    )
    drifts = exchange(drifts.reshape(32, 32, C), TM).reshape(CELLS, C)
    (sums,) = call(
        sum_kernel, [struct((CELLS, C), F32)], (drifts, noise_before), [], False, 2 * CELLS * C
    )
    sums = exchange(sums.reshape(512, 2, C), ALL).reshape(SIDE, SIDE, C)
    advanced = start + (sums + coefficient * time_value * noise)
    return advanced[None, None]


def solution(mesh):
    finer = Mesh(mesh.devices.reshape(4, 8, mesh.shape["frame"]), ALL)
    placed = (
        P("frame", None, None, None),
        P(TM, "frame", None, None, None),
        P(TM, "frame", None, None, None),
        P(TM),
        P(),
        P(),
        P(),
        P(),
        P(),
        P(),
    )
    return jax.shard_map(
        shards,
        mesh=finer,
        in_specs=placed,
        out_specs=P(TM, "frame", None, None, None),
        check_vma=False,
    )
```

```python
import math

import jax
import jax.numpy as jnp
from jax import lax
from jax.experimental import pallas as pl
from jax.experimental.pallas import tpu as pltpu
from jax.sharding import Mesh
from jax.sharding import PartitionSpec as P

C = 128
HEAD_DIM = 64
FRAMES = 16
STEPS = 32
SIDE = 32
CELLS = SIDE * SIDE
TM = ("tm_0", "tm_1")
ALL = ("tm_0", "tm_1", "frame")
F32 = jnp.float32
BF16 = jnp.bfloat16
VMEM = pl.BlockSpec(memory_space=pltpu.VMEM)
SMEM = pl.BlockSpec(memory_space=pltpu.SMEM)


def dot(left, right):
    return jnp.dot(left, right, preferred_element_type=F32)


def unit(field, gain):
    return field * lax.rsqrt(jnp.mean(field * field, axis=-1, keepdims=True) + 1e-06) * gain


def attention_masks():
    row = lax.broadcasted_iota(jnp.int32, (128, 128), 0)
    lane = lax.broadcasted_iota(jnp.int32, (128, 128), 1)
    return row // FRAMES == lane // FRAMES, lane < HEAD_DIM


def attend_block(mixed, gain, attention_weight, output_weight, masks):
    same_cell, first_head = masks
    projected = dot(unit(mixed, gain).astype(BF16), attention_weight).astype(BF16)
    queries, keys, values = (projected[:, i * C : (i + 1) * C] for i in range(3))
    zero = jnp.zeros((), BF16)
    attended = None
    for head in range(2):
        lanes = first_head if head == 0 else jnp.logical_not(first_head)
        scores = lax.dot_general(
            jnp.where(lanes, queries, zero), keys, (((1,), (1,)), ((), ())), preferred_element_type=F32
        ) * (1.0 / math.sqrt(HEAD_DIM))
        scores = jnp.where(same_cell, scores, -1e30)
        grown = jnp.exp(scores - jnp.max(scores, axis=-1, keepdims=True))
        weights = (grown * (1.0 / jnp.sum(grown, axis=-1, keepdims=True))).astype(BF16)
        part = dot(weights, jnp.where(lanes, values, zero))
        attended = part if attended is None else attended + part
    return dot(attended.astype(BF16), output_weight)


def first_kernel(
    scalars, guess, noise, start, gain, scaling, offset, space_weight, out, padded, plain, packed
):
    col = lax.broadcasted_iota(jnp.int32, (8, SIDE, C), 1)
    padded[0] = jnp.zeros((SIDE, 3 * C), BF16)
    padded[SIDE + 1] = jnp.zeros((SIDE, 3 * C), BF16)
    for block in range(4):
        rows = pl.ds(block * 8, 8)
        state = guess[rows]
        normed = unit(state, gain[...]) * scaling[...] + offset[...]
        left = jnp.where(col == 0, 0.0, pltpu.roll(normed, 1, 1))
        right = jnp.where(col == SIDE - 1, 0.0, pltpu.roll(normed, SIDE - 1, 1))
        at = pl.ds(block * 8 + 1, 8)
        padded[at, :, 0:C] = left.astype(BF16)
        padded[at, :, C : 2 * C] = normed.astype(BF16)
        padded[at, :, 2 * C : 3 * C] = right.astype(BF16)
    total = None
    for shift in range(3):
        part = dot(
            padded[shift : shift + SIDE].reshape(CELLS, 3 * C),
            space_weight[shift * 3 * C : (shift + 1) * 3 * C, :],
        )
        total = part if total is None else total + part
    plain[...] = total
    scale = scalars[0]
    last = scalars[1] > 0.5
    for block in range(8):
        rows = pl.ds(block * 128, 128)
        conv = plain[rows, :]
        mixed = guess[pl.ds(block * 4, 4)].reshape(128, C) + conv * jax.nn.sigmoid(conv)
        begun = start[pl.ds(block * 4, 4)].reshape(128, C)
        begun_high = begun.astype(BF16).astype(F32)
        plain[rows, :] = jnp.where(last, begun - begun_high, mixed)
        drawn = noise[pl.ds(block * 4, 4)].reshape(128, C) * scale
        packed[pl.ds(CELLS + block * 128, 128), :] = jnp.where(last, begun_high, drawn)
    for block in range(8):
        half = CELLS // 16
        for slot in range(4):
            if slot < 2:
                piece = plain[pl.ds(block * 128 + slot, half, 2), :]
            else:
                piece = packed[pl.ds(CELLS + block * 128 + slot - 2, half, 2), :]
            packed[pl.ds(2 * CELLS + slot, half, 4), :] = piece
        out[pl.ds(block * 256, 256), :] = packed[pl.ds(2 * CELLS, 256), :].astype(BF16)


def owner_kernel(coefficients, received, gain, attention_weight, output_weight, states, noise_before, wide, drifts):
    masks = attention_masks()
    wide[...] = received[...].astype(F32)
    for cell in range(2):
        for block in range(4):
            mixed = wide[pl.ds(block * 512 + cell, 128, 4), :]
            drifts[pl.ds(cell * 512 + block * 128, 128), :] = mixed + attend_block(
                mixed, gain[...], attention_weight[...], output_weight[...], masks
            )
    for cell in range(2):
        tail = (STEPS - 1) * FRAMES * 4 + cell
        state = wide[pl.ds(tail + 2, FRAMES, 4), :] + wide[pl.ds(tail, FRAMES, 4), :]
        noises = jnp.zeros((FRAMES, C), F32)
        for step in range(STEPS):
            rows = pl.ds(step * 32 + cell * FRAMES, FRAMES)
            states[rows, :] = state.astype(BF16)
            noise_before[rows, :] = noises
            if step < STEPS - 1:
                drawn = wide[pl.ds(step * FRAMES * 4 + 2 + cell, FRAMES, 4), :]
                drift = drifts[pl.ds(cell * 512 + step * FRAMES, FRAMES), :]
                state = state + (coefficients[step : step + 1, :] * drift + drawn)
                noises = noises + drawn


def norm_kernel(state, gain, scaling, offset, first, second):
    for cell, out in ((0, first), (1, second)):
        for block in range(4):
            rows = state[pl.ds(block * 8, 8), cell].astype(F32)
            normed = unit(rows, gain[...]) * scaling[...] + offset[...]
            out[pl.ds(block * 8, 8)] = normed.astype(BF16)


def second_kernel(
    scalars, state, left, first, second, right, space_weight, gain, attention_weight, output_weight, out, padded, conv
):
    for col, piece in enumerate((left, first, second, right)):
        padded[col, 0] = jnp.zeros((FRAMES, C), BF16)
        padded[col, SIDE + 1] = jnp.zeros((FRAMES, C), BF16)
        padded[col, 1 : SIDE + 1] = piece[...]
    for cell in range(2):
        taps = [
            padded[cell + across, down : down + SIDE].reshape(SIDE * FRAMES, C)
            for down in range(3)
            for across in range(3)
        ]
        conv[cell] = dot(jnp.concatenate(taps, axis=-1), space_weight[...])
    masks = attention_masks()
    coefficient = scalars[2]
    for cell in range(2):
        for block in range(4):
            found = conv[cell, pl.ds(block * 128, 128), :]
            here = state[pl.ds(block * 8, 8), cell].reshape(128, C).astype(F32)
            mixed = here + found * jax.nn.sigmoid(found)
            drift = mixed + attend_block(
                mixed, gain[...], attention_weight[...], output_weight[...], masks
            )
            out[pl.ds(block * 8, 8), cell] = (coefficient * drift).reshape(8, FRAMES, C).astype(BF16)


def sum_kernel(received, noise_before, out):
    for cell in range(2):
        total = jnp.zeros((FRAMES, C), F32)
        for step in range(STEPS):
            rows = pl.ds(step * 32 + cell * FRAMES, FRAMES)
            total = total + received[rows, :].astype(F32)
            out[pl.ds(step * 32 + cell, FRAMES, 2), :] = total + noise_before[rows, :]


def call(kernel, outs, operands, scratch, scalar_first, flops):
    specs = [SMEM if scalar_first and i == 0 else VMEM for i in range(len(operands))]
    moved = sum(x.size * x.dtype.itemsize for x in (*operands, *outs))
    return pl.pallas_call(
        kernel,
        out_shape=outs,
        in_specs=specs,
        out_specs=[VMEM] * len(outs),
        scratch_shapes=scratch,
        compiler_params=pltpu.CompilerParams(vmem_limit_bytes=16 << 20),
        cost_estimate=pl.CostEstimate(flops=flops, bytes_accessed=moved, transcendentals=0),
    )(*operands)


def struct(shape, dtype):
    return jax.ShapeDtypeStruct(shape, dtype)


def embed_time(step_value):
    half_width = C // 2
    frequency = jnp.exp(-math.log(10000.0) * jnp.arange(half_width, dtype=F32) / half_width)
    angles = step_value.astype(F32) * frequency
    return jnp.concatenate([jnp.cos(angles), jnp.sin(angles)])


def modulation(step_value, time_weight):
    encoded = embed_time(step_value)[None, :]
    shifted = jnp.dot(encoded, time_weight, precision=lax.Precision.HIGHEST, preferred_element_type=F32)
    return (1.0 + shifted[:, :C], shifted[:, C:])


def exchange(array, axes):
    return lax.all_to_all(array, axes, 0, 0, tiled=True)


def shards(
    start_state,
    initial_guess,
    noise_draws,
    timesteps,
    gain_space,
    gain_attention,
    time_weight,
    space_weight,
    attention_weight,
    output_weight,
):
    steps_total = lax.axis_size(TM)
    step_value = timesteps[0]
    time_value = step_value.astype(F32) / 1000.0
    coefficient = (0.5 + time_value) / math.sqrt(steps_total)
    scaling, offset = modulation(step_value, time_weight)
    guess, noise, start = initial_guess[0, 0], noise_draws[0, 0], start_state[0]
    gain_s, gain_a = gain_space[None, :], gain_attention[None, :]
    is_last = (lax.axis_index(TM) == steps_total - 1).astype(F32)
    scalars = jnp.stack([coefficient * time_value, is_last, coefficient])

    (sent,) = call(
        first_kernel,
        [struct((2 * CELLS, C), BF16)],
        (scalars, guess, noise, start, gain_s, scaling, offset, space_weight),
        [
            pltpu.VMEM((SIDE + 2, SIDE, 3 * C), BF16),
            pltpu.VMEM((CELLS, C), F32),
            pltpu.VMEM((2 * CELLS + 256, C), F32),
        ],
        True,
        2 * CELLS * 9 * C * C,
    )
    received = exchange(sent.reshape(512, 4, C), ALL).reshape(2 * CELLS, C)
    coefficients = exchange(jnp.broadcast_to(coefficient, (steps_total, 1, C)), TM).reshape(steps_total, C)
    states, noise_before = call(
        owner_kernel,
        [struct((CELLS, C), BF16), struct((CELLS, C), F32)],
        (coefficients, received, gain_a, attention_weight, output_weight),
        [pltpu.VMEM((2 * CELLS, C), F32), pltpu.VMEM((CELLS, C), F32)],
        False,
        2 * CELLS * 8 * C * C,
    )
    state = exchange(states.reshape(32, 32, C), TM).reshape(SIDE, 2, FRAMES, C)
    first, second = call(
        norm_kernel,
        [struct((SIDE, FRAMES, C), BF16)] * 2,
        (state, gain_s, scaling, offset),
        [],
        False,
        10 * CELLS * C,
    )
    count = lax.axis_size("frame")
    left = lax.ppermute(second, "frame", [(k, k + 1) for k in range(count - 1)])
    right = lax.ppermute(first, "frame", [(k + 1, k) for k in range(count - 1)])
    (drifts,) = call(
        second_kernel,
        [struct((SIDE, 2, FRAMES, C), BF16)],
        (scalars, state, left, first, second, right, space_weight, gain_a, attention_weight, output_weight),
        [pltpu.VMEM((4, SIDE + 2, FRAMES, C), BF16), pltpu.VMEM((2, CELLS // 2, C), F32)],
        True,
        2 * CELLS * 17 * C * C,
    )
    drifts = exchange(drifts.reshape(32, 32, C), TM).reshape(CELLS, C)
    (sums,) = call(
        sum_kernel, [struct((CELLS, C), F32)], (drifts, noise_before), [], False, 2 * CELLS * C
    )
    sums = exchange(sums.reshape(512, 2, C), ALL).reshape(SIDE, SIDE, C)
    advanced = start + (sums + coefficient * time_value * noise)
    return advanced[None, None]


def solution(mesh):
    finer = Mesh(mesh.devices.reshape(4, 8, mesh.shape["frame"]), ALL)
    placed = (
        P("frame", None, None, None),
        P(TM, "frame", None, None, None),
        P(TM, "frame", None, None, None),
        P(TM),
        P(),
        P(),
        P(),
        P(),
        P(),
        P(),
    )
    return jax.shard_map(
        shards,
        mesh=finer,
        in_specs=placed,
        out_specs=P(TM, "frame", None, None, None),
        check_vma=False,
    )
```

```python
import math

import jax
import jax.numpy as jnp
from jax import lax
from jax.experimental import pallas as pl
from jax.experimental.pallas import tpu as pltpu
from jax.sharding import Mesh
from jax.sharding import PartitionSpec as P

C = 128
HEAD_DIM = 64
FRAMES = 16
STEPS = 32
SIDE = 32
CELLS = SIDE * SIDE
TM = ("tm_0", "tm_1")
ALL = ("tm_0", "tm_1", "frame")
F32 = jnp.float32
BF16 = jnp.bfloat16
VMEM = pl.BlockSpec(memory_space=pltpu.VMEM)
SMEM = pl.BlockSpec(memory_space=pltpu.SMEM)
FAR = pl.BlockSpec(memory_space=pltpu.HBM)


def dot(left, right):
    return jnp.dot(left, right, preferred_element_type=F32)


def unit(field, gain):
    return field * lax.rsqrt(jnp.mean(field * field, axis=-1, keepdims=True) + 1e-06) * gain


def attention_masks(cell_major):
    row = lax.broadcasted_iota(jnp.int32, (128, 128), 0)
    lane = lax.broadcasted_iota(jnp.int32, (128, 128), 1)
    same_cell = row // FRAMES == lane // FRAMES if cell_major else row % 8 == lane % 8
    return same_cell, lane < HEAD_DIM


def attend_block(mixed, gain, attention_weight, output_weight, masks):
    same_cell, first_head = masks
    projected = dot(unit(mixed, gain).astype(BF16), attention_weight).astype(BF16)
    queries, keys, values = (projected[:, i * C : (i + 1) * C] for i in range(3))
    zero = jnp.zeros((), BF16)
    attended = None
    for head in range(2):
        lanes = first_head if head == 0 else jnp.logical_not(first_head)
        scores = lax.dot_general(
            jnp.where(lanes, queries, zero), keys, (((1,), (1,)), ((), ())), preferred_element_type=F32
        ) * (1.0 / math.sqrt(HEAD_DIM))
        scores = jnp.where(same_cell, scores, -1e30)
        grown = jnp.exp(scores - jnp.max(scores, axis=-1, keepdims=True))
        weights = (grown * (1.0 / jnp.sum(grown, axis=-1, keepdims=True))).astype(BF16)
        part = dot(weights, jnp.where(lanes, values, zero))
        attended = part if attended is None else attended + part
    return dot(attended.astype(BF16), output_weight)


def first_kernel(
    scalars, guess_far, noise_far, start_far, weight_far, gain, scaling, offset, out,
    guess, noise, start, space_weight, padded, mixed, drawn, sems,
):
    copies = [
        pltpu.make_async_copy(far, near, sems.at[i])
        for i, (far, near) in enumerate(
            ((guess_far, guess), (weight_far, space_weight), (noise_far, noise), (start_far, start))
        )
    ]
    for copy in copies:
        copy.start()
    col = lax.broadcasted_iota(jnp.int32, (8, SIDE, C), 1)
    padded[0] = jnp.zeros((SIDE, 3 * C), BF16)
    padded[SIDE + 1] = jnp.zeros((SIDE, 3 * C), BF16)
    copies[0].wait()
    for block in range(4):
        rows = pl.ds(block * 8, 8)
        state = guess[rows]
        normed = unit(state, gain[...]) * scaling[...] + offset[...]
        left = jnp.where(col == 0, 0.0, pltpu.roll(normed, 1, 1))
        right = jnp.where(col == SIDE - 1, 0.0, pltpu.roll(normed, SIDE - 1, 1))
        at = pl.ds(block * 8 + 1, 8)
        padded[at, :, 0:C] = left.astype(BF16)
        padded[at, :, C : 2 * C] = normed.astype(BF16)
        padded[at, :, 2 * C : 3 * C] = right.astype(BF16)
    copies[1].wait()
    total = None
    for shift in range(3):
        part = dot(
            padded[shift : shift + SIDE].reshape(CELLS, 3 * C),
            space_weight[shift * 3 * C : (shift + 1) * 3 * C, :],
        )
        total = part if total is None else total + part
    mixed[...] = total
    copies[2].wait()
    copies[3].wait()
    scale = scalars[0]
    last = scalars[1] > 0.5
    for block in range(8):
        rows = pl.ds(block * 128, 128)
        band = pl.ds(block * 4, 4)
        conv = mixed[rows, :]
        here = guess[band].reshape(128, C) + conv * jax.nn.sigmoid(conv)
        begun = start[band].reshape(128, C)
        begun_high = begun.astype(BF16).astype(F32)
        mixed[rows, :] = jnp.where(last, begun - begun_high, here)
        drawn[rows, :] = jnp.where(last, begun_high, noise[band].reshape(128, C) * scale)
    for holder in range(FRAMES):
        for slot, source in enumerate((mixed, drawn)):
            for side in range(2):
                piece = source[pl.ds(2 * holder + side, SIDE, SIDE), :]
                out[holder, pl.ds(slot * 64 + side * SIDE, SIDE), :] = piece.astype(BF16)


def holder_kernel(scalars, received, gain, attention_weight, output_weight, terms, noises, wide, turned, turned_noise):
    masks = attention_masks(False)
    wide[...] = received[...].astype(F32)
    last = scalars[1] > 0.5
    coefficient = scalars[2]
    for side in range(2):
        for block in range(4):
            first = side * SIDE + block * 8
            mixed = wide[:, first : first + 8, :].reshape(128, C)
            drawn = wide[:, 64 + first : 64 + first + 8, :].reshape(128, C)
            drift = mixed + attend_block(
                mixed, gain[...], attention_weight[...], output_weight[...], masks
            )
            turned[...] = jnp.where(last, mixed + drawn, coefficient * drift + drawn)
            turned_noise[...] = jnp.where(last, 0.0, drawn)
            for j in range(8):
                rows = pl.ds(((block * 8 + j) * 2 + side) * FRAMES, FRAMES)
                terms[rows, :] = turned[pl.ds(j, FRAMES, 8), :]
                noises[rows, :] = turned_noise[pl.ds(j, FRAMES, 8), :]


def before_kernel(received, states):
    for half in range(2):
        state = received[pl.ds((STEPS - 1) * 32 + half * 16, 16), :]
        for step in range(STEPS):
            rows = pl.ds(step * 32 + half * 16, 16)
            states[rows, :] = state.astype(BF16)
            state = state + received[rows, :]


def norm_kernel(state, gain, scaling, offset, first, second):
    for cell, out in ((0, first), (1, second)):
        for block in range(4):
            rows = state[pl.ds(block * 8, 8), cell].astype(F32)
            normed = unit(rows, gain[...]) * scaling[...] + offset[...]
            out[pl.ds(block * 8, 8)] = normed.astype(BF16)


def second_kernel(
    scalars, state, left, first, second, right, noises, space_weight, gain, attention_weight, output_weight, out, padded, conv
):
    for col, piece in enumerate((left, first, second, right)):
        padded[col, 0] = jnp.zeros((FRAMES, C), BF16)
        padded[col, SIDE + 1] = jnp.zeros((FRAMES, C), BF16)
        padded[col, 1 : SIDE + 1] = piece[...]
    for cell in range(2):
        taps = [
            padded[cell + across, down : down + SIDE].reshape(SIDE * FRAMES, C)
            for down in range(3)
            for across in range(3)
        ]
        conv[cell] = dot(jnp.concatenate(taps, axis=-1), space_weight[...])
    masks = attention_masks(True)
    coefficient = scalars[2]
    for cell in range(2):
        for block in range(4):
            found = conv[cell, pl.ds(block * 128, 128), :]
            here = state[pl.ds(block * 8, 8), cell].reshape(128, C).astype(F32)
            mixed = here + found * jax.nn.sigmoid(found)
            drift = mixed + attend_block(
                mixed, gain[...], attention_weight[...], output_weight[...], masks
            )
            term = coefficient * drift + noises[pl.ds(block * 8, 8), cell].reshape(128, C)
            out[pl.ds(block * 8, 8), cell] = term.reshape(8, FRAMES, C).astype(BF16)


def sum_kernel(received, out):
    for cell in range(2):
        total = jnp.zeros((FRAMES, C), F32)
        for step in range(STEPS):
            rows = pl.ds(step * 32 + cell * FRAMES, FRAMES)
            total = total + received[rows, :].astype(F32)
            out[pl.ds(step * 32 + cell, FRAMES, 2), :] = total


def call(kernel, outs, operands, scratch, flops, spaces=(), grant=16):
    specs = [*spaces, *[VMEM] * (len(operands) - len(spaces))]
    moved = sum(x.size * x.dtype.itemsize for x in (*operands, *outs))
    return pl.pallas_call(
        kernel,
        out_shape=outs,
        in_specs=specs,
        out_specs=[VMEM] * len(outs),
        scratch_shapes=scratch,
        compiler_params=pltpu.CompilerParams(vmem_limit_bytes=grant << 20),
        cost_estimate=pl.CostEstimate(flops=flops, bytes_accessed=moved, transcendentals=0),
    )(*operands)


def struct(shape, dtype):
    return jax.ShapeDtypeStruct(shape, dtype)


def embed_time(step_value):
    half_width = C // 2
    frequency = jnp.exp(-math.log(10000.0) * jnp.arange(half_width, dtype=F32) / half_width)
    angles = step_value.astype(F32) * frequency
    return jnp.concatenate([jnp.cos(angles), jnp.sin(angles)])


def modulation(step_value, time_weight):
    encoded = embed_time(step_value)[None, :]
    shifted = jnp.dot(encoded, time_weight, precision=lax.Precision.HIGHEST, preferred_element_type=F32)
    return (1.0 + shifted[:, :C], shifted[:, C:])


def exchange(array, axes):
    return lax.all_to_all(array, axes, 0, 0, tiled=True)


def shards(
    start_state,
    initial_guess,
    noise_draws,
    timesteps,
    gain_space,
    gain_attention,
    time_weight,
    space_weight,
    attention_weight,
    output_weight,
):
    steps_total = lax.axis_size(TM)
    step_value = timesteps[0]
    time_value = step_value.astype(F32) / 1000.0
    coefficient = (0.5 + time_value) / math.sqrt(steps_total)
    scaling, offset = modulation(step_value, time_weight)
    guess, noise, start = initial_guess[0, 0], noise_draws[0, 0], start_state[0]
    gain_s, gain_a = gain_space[None, :], gain_attention[None, :]
    is_last = (lax.axis_index(TM) == steps_total - 1).astype(F32)
    noise_scale = coefficient * time_value
    scalars = jnp.stack([noise_scale, is_last, coefficient])
    scalars, own_scale = lax.optimization_barrier((scalars, is_last * noise_scale))

    (sent,) = call(
        first_kernel,
        [struct((FRAMES, 128, C), BF16)],
        (scalars, guess, noise, start, space_weight, gain_s, scaling, offset),
        [
            pltpu.VMEM((SIDE, SIDE, C), F32),
            pltpu.VMEM((SIDE, SIDE, C), F32),
            pltpu.VMEM((SIDE, SIDE, C), F32),
            pltpu.VMEM((9 * C, C), BF16),
            pltpu.VMEM((SIDE + 2, SIDE, 3 * C), BF16),
            pltpu.VMEM((CELLS, C), F32),
            pltpu.VMEM((CELLS, C), F32),
            pltpu.SemaphoreType.DMA((4,)),
        ],
        2 * CELLS * 9 * C * C,
        (SMEM, FAR, FAR, FAR, FAR),
        62,
    )
    terms, noises = call(
        holder_kernel,
        [struct((CELLS, C), F32), struct((CELLS, C), F32)],
        (scalars, exchange(sent, "frame"), gain_a, attention_weight, output_weight),
        [pltpu.VMEM((FRAMES, 128, C), F32), pltpu.VMEM((128, C), F32), pltpu.VMEM((128, C), F32)],
        2 * CELLS * 8 * C * C,
        (SMEM,),
    )
    terms = exchange(terms.reshape(32, 32, C), TM).reshape(CELLS, C)
    (states,) = call(before_kernel, [struct((CELLS, C), BF16)], (terms,), [], 2 * CELLS * C)
    state = exchange(states.reshape(32, 32, C), TM).reshape(SIDE, 2, FRAMES, C)
    first, second = call(
        norm_kernel,
        [struct((SIDE, FRAMES, C), BF16)] * 2,
        (state, gain_s, scaling, offset),
        [],
        10 * CELLS * C,
    )
    count = lax.axis_size("frame")
    left = lax.ppermute(second, "frame", [(k, k + 1) for k in range(count - 1)])
    right = lax.ppermute(first, "frame", [(k + 1, k) for k in range(count - 1)])
    noises = noises.reshape(SIDE, 2, FRAMES, C)
    (terms,) = call(
        second_kernel,
        [struct((SIDE, 2, FRAMES, C), BF16)],
        (scalars, state, left, first, second, right, noises, space_weight, gain_a, attention_weight, output_weight),
        [pltpu.VMEM((4, SIDE + 2, FRAMES, C), BF16), pltpu.VMEM((2, CELLS // 2, C), F32)],
        2 * CELLS * 17 * C * C,
        (SMEM,),
    )
    terms = exchange(terms.reshape(32, 32, C), TM).reshape(CELLS, C)
    (sums,) = call(sum_kernel, [struct((CELLS, C), F32)], (terms,), [], 2 * CELLS * C)
    sums = exchange(sums.reshape(512, 2, C), ALL).reshape(SIDE, SIDE, C)
    advanced = start + (sums + own_scale * noise)
    return advanced[None, None]


def solution(mesh):
    finer = Mesh(mesh.devices.reshape(4, 8, mesh.shape["frame"]), ALL)
    placed = (
        P("frame", None, None, None),
        P(TM, "frame", None, None, None),
        P(TM, "frame", None, None, None),
        P(TM),
        P(),
        P(),
        P(),
        P(),
        P(),
        P(),
    )
    return jax.shard_map(
        shards,
        mesh=finer,
        in_specs=placed,
        out_specs=P(TM, "frame", None, None, None),
        check_vma=False,
    )
```

```python
import math

import jax
import jax.numpy as jnp
from jax import lax
from jax.experimental import pallas as pl
from jax.experimental.pallas import tpu as pltpu
from jax.sharding import Mesh
from jax.sharding import PartitionSpec as P

C = 128
HEAD_DIM = 64
FRAMES = 16
STEPS = 32
SIDE = 32
CELLS = SIDE * SIDE
TM = ("tm_0", "tm_1")
ALL = ("tm_0", "tm_1", "frame")
F32 = jnp.float32
BF16 = jnp.bfloat16
VMEM = pl.BlockSpec(memory_space=pltpu.VMEM)
SMEM = pl.BlockSpec(memory_space=pltpu.SMEM)
FAR = pl.BlockSpec(memory_space=pltpu.HBM)


def dot(left, right):
    return jnp.dot(left, right, preferred_element_type=F32)


def unit(field, gain):
    return field * lax.rsqrt(jnp.mean(field * field, axis=-1, keepdims=True) + 1e-06) * gain


def attention_masks(cell_major):
    row = lax.broadcasted_iota(jnp.int32, (128, 128), 0)
    lane = lax.broadcasted_iota(jnp.int32, (128, 128), 1)
    same_cell = row // FRAMES == lane // FRAMES if cell_major else row % 8 == lane % 8
    return same_cell, lane < HEAD_DIM


def attend_block(mixed, gain, attention_weight, output_weight, masks):
    same_cell, first_head = masks
    projected = dot(unit(mixed, gain).astype(BF16), attention_weight).astype(BF16)
    queries, keys, values = (projected[:, i * C : (i + 1) * C] for i in range(3))
    zero = jnp.zeros((), BF16)
    attended = None
    for head in range(2):
        lanes = first_head if head == 0 else jnp.logical_not(first_head)
        scores = lax.dot_general(
            jnp.where(lanes, queries, zero), keys, (((1,), (1,)), ((), ())), preferred_element_type=F32
        ) * (1.0 / math.sqrt(HEAD_DIM))
        scores = jnp.where(same_cell, scores, -1e30)
        grown = jnp.exp(scores - jnp.max(scores, axis=-1, keepdims=True))
        weights = (grown * (1.0 / jnp.sum(grown, axis=-1, keepdims=True))).astype(BF16)
        part = dot(weights, jnp.where(lanes, values, zero))
        attended = part if attended is None else attended + part
    return dot(attended.astype(BF16), output_weight)


def first_kernel(
    scalars, guess_far, noise_far, start_far, weight_far, gain, scaling, offset, out,
    guess, noise, start, space_weight, padded, mixed, drawn, packed, sems,
):
    copies = [
        pltpu.make_async_copy(far, near, sems.at[i])
        for i, (far, near) in enumerate(
            ((guess_far, guess), (weight_far, space_weight), (noise_far, noise), (start_far, start))
        )
    ]
    for copy in copies:
        copy.start()
    col = lax.broadcasted_iota(jnp.int32, (8, SIDE, C), 1)
    padded[0] = jnp.zeros((SIDE, 3 * C), BF16)
    padded[SIDE + 1] = jnp.zeros((SIDE, 3 * C), BF16)
    copies[0].wait()
    for block in range(4):
        rows = pl.ds(block * 8, 8)
        state = guess[rows]
        normed = unit(state, gain[...]) * scaling[...] + offset[...]
        left = jnp.where(col == 0, 0.0, pltpu.roll(normed, 1, 1))
        right = jnp.where(col == SIDE - 1, 0.0, pltpu.roll(normed, SIDE - 1, 1))
        at = pl.ds(block * 8 + 1, 8)
        padded[at, :, 0:C] = left.astype(BF16)
        padded[at, :, C : 2 * C] = normed.astype(BF16)
        padded[at, :, 2 * C : 3 * C] = right.astype(BF16)
    copies[1].wait()
    total = None
    for shift in range(3):
        part = dot(
            padded[shift : shift + SIDE].reshape(CELLS, 3 * C),
            space_weight[shift * 3 * C : (shift + 1) * 3 * C, :],
        )
        total = part if total is None else total + part
    mixed[...] = total
    copies[2].wait()
    copies[3].wait()
    scale = scalars[0]
    last = scalars[1] > 0.5
    for block in range(8):
        rows = pl.ds(block * 128, 128)
        band = pl.ds(block * 4, 4)
        conv = mixed[rows, :]
        here = guess[band].reshape(128, C) + conv * jax.nn.sigmoid(conv)
        begun = start[band].reshape(128, C)
        begun_high = begun.astype(BF16).astype(F32)
        mixed[rows, :] = jnp.where(last, begun - begun_high, here)
        drawn[rows, :] = jnp.where(last, begun_high, noise[band].reshape(128, C) * scale)
    for block in range(8):
        half = CELLS // 16
        for slot, source in enumerate((mixed, mixed, drawn, drawn)):
            packed[pl.ds(block * 256 + slot, half, 4), :] = source[pl.ds(block * 128 + slot % 2, half, 2), :]
        rows = pl.ds(block * 256, 256)
        out[rows, :] = packed[rows, :].astype(BF16)


def owner_kernel(all_steps, received, gain, attention_weight, output_weight, states, wide, drifts):
    masks = attention_masks(True)
    wide[...] = received[...].astype(F32)
    for cell in range(2):
        for block in range(4):
            mixed = wide[pl.ds(block * 512 + cell, 128, 4), :]
            drifts[pl.ds(cell * 512 + block * 128, 128), :] = mixed + attend_block(
                mixed, gain[...], attention_weight[...], output_weight[...], masks
            )
    for cell in range(2):
        tail = (STEPS - 1) * FRAMES * 4 + cell
        state = wide[pl.ds(tail + 2, FRAMES, 4), :] + wide[pl.ds(tail, FRAMES, 4), :]
        for step in range(STEPS):
            states[pl.ds(step * 32 + cell * FRAMES, FRAMES), :] = state.astype(BF16)
            if step < STEPS - 1:
                drawn = wide[pl.ds(step * FRAMES * 4 + 2 + cell, FRAMES, 4), :]
                drift = drifts[pl.ds(cell * 512 + step * FRAMES, FRAMES), :]
                coefficient = (0.5 + all_steps[step].astype(F32) / 1000.0) / math.sqrt(STEPS)
                state = state + (coefficient * drift + drawn)


def norm_kernel(state, gain, scaling, offset, first, second):
    for cell, out in ((0, first), (1, second)):
        for block in range(4):
            rows = state[pl.ds(block * 8, 8), cell].astype(F32)
            normed = unit(rows, gain[...]) * scaling[...] + offset[...]
            out[pl.ds(block * 8, 8)] = normed.astype(BF16)


def second_kernel(
    scalars, state, left, first, second, right, space_weight, gain, attention_weight, output_weight, out, padded, conv, block_out, turned
):
    for col, piece in enumerate((left, first, second, right)):
        padded[col, 0] = jnp.zeros((FRAMES, C), BF16)
        padded[col, SIDE + 1] = jnp.zeros((FRAMES, C), BF16)
        padded[col, 1 : SIDE + 1] = piece[...]
    for cell in range(2):
        taps = [
            padded[cell + across, down : down + SIDE].reshape(SIDE * FRAMES, C)
            for down in range(3)
            for across in range(3)
        ]
        conv[cell] = dot(jnp.concatenate(taps, axis=-1), space_weight[...])
    masks = attention_masks(True)
    coefficient = scalars[2]
    for cell in range(2):
        for block in range(4):
            found = conv[cell, pl.ds(block * 128, 128), :]
            here = state[pl.ds(block * 8, 8), cell].reshape(128, C).astype(F32)
            mixed = here + found * jax.nn.sigmoid(found)
            drift = mixed + attend_block(
                mixed, gain[...], attention_weight[...], output_weight[...], masks
            )
            block_out[...] = coefficient * drift
            for frame in range(FRAMES):
                turned[frame, pl.ds(cell * SIDE + block * 8, 8), :] = block_out[pl.ds(frame, 8, FRAMES), :]
    out[...] = turned[...].astype(BF16)


def frame_kernel(scalars, received, noise, out, natural):
    for holder in range(FRAMES):
        for side in range(2):
            piece = received[holder, pl.ds(side * SIDE, SIDE), :].astype(F32)
            natural[pl.ds(2 * holder + side, SIDE, SIDE), :] = piece
    out[...] = (natural[...] + scalars[0] * noise[...]).astype(BF16)


def sum_kernel(received, out):
    for half in range(2):
        total = jnp.zeros((FRAMES, C), F32)
        for step in range(STEPS):
            rows = pl.ds(step * 32 + half * FRAMES, FRAMES)
            total = total + received[rows, :].astype(F32)
            out[rows, :] = total


def call(kernel, outs, operands, scratch, flops, spaces=(), grant=16):
    specs = [*spaces, *[VMEM] * (len(operands) - len(spaces))]
    moved = sum(x.size * x.dtype.itemsize for x in (*operands, *outs))
    return pl.pallas_call(
        kernel,
        out_shape=outs,
        in_specs=specs,
        out_specs=[VMEM] * len(outs),
        scratch_shapes=scratch,
        compiler_params=pltpu.CompilerParams(vmem_limit_bytes=grant << 20),
        cost_estimate=pl.CostEstimate(flops=flops, bytes_accessed=moved, transcendentals=0),
    )(*operands)


def struct(shape, dtype):
    return jax.ShapeDtypeStruct(shape, dtype)


def embed_time(step_value):
    half_width = C // 2
    frequency = jnp.exp(-math.log(10000.0) * jnp.arange(half_width, dtype=F32) / half_width)
    angles = step_value.astype(F32) * frequency
    return jnp.concatenate([jnp.cos(angles), jnp.sin(angles)])


def modulation(step_value, time_weight):
    encoded = embed_time(step_value)[None, :]
    shifted = jnp.dot(encoded, time_weight, precision=lax.Precision.HIGHEST, preferred_element_type=F32)
    return (1.0 + shifted[:, :C], shifted[:, C:])


def exchange(array, axes):
    return lax.all_to_all(array, axes, 0, 0, tiled=True)


def shards(
    start_state,
    initial_guess,
    noise_draws,
    timesteps,
    gain_space,
    gain_attention,
    time_weight,
    space_weight,
    attention_weight,
    output_weight,
):
    steps_total = lax.axis_size(TM)
    step_value = timesteps[0]
    time_value = step_value.astype(F32) / 1000.0
    coefficient = (0.5 + time_value) / math.sqrt(steps_total)
    scaling, offset = modulation(step_value, time_weight)
    guess, noise, start = initial_guess[0, 0], noise_draws[0, 0], start_state[0]
    gain_s, gain_a = gain_space[None, :], gain_attention[None, :]
    is_last = (lax.axis_index(TM) == steps_total - 1).astype(F32)
    scalars = jnp.stack([coefficient * time_value, is_last, coefficient])

    (sent,) = call(
        first_kernel,
        [struct((2 * CELLS, C), BF16)],
        (scalars, guess, noise, start, space_weight, gain_s, scaling, offset),
        [
            pltpu.VMEM((SIDE, SIDE, C), F32),
            pltpu.VMEM((SIDE, SIDE, C), F32),
            pltpu.VMEM((SIDE, SIDE, C), F32),
            pltpu.VMEM((9 * C, C), BF16),
            pltpu.VMEM((SIDE + 2, SIDE, 3 * C), BF16),
            pltpu.VMEM((CELLS, C), F32),
            pltpu.VMEM((CELLS, C), F32),
            pltpu.VMEM((2 * CELLS, C), F32),
            pltpu.SemaphoreType.DMA((4,)),
        ],
        2 * CELLS * 9 * C * C,
        (SMEM, FAR, FAR, FAR, FAR),
        62,
    )
    received = exchange(sent.reshape(512, 4, C), ALL).reshape(2 * CELLS, C)
    all_steps = lax.all_gather(timesteps, TM, tiled=True)
    (states,) = call(
        owner_kernel,
        [struct((CELLS, C), BF16)],
        (all_steps, received, gain_a, attention_weight, output_weight),
        [pltpu.VMEM((2 * CELLS, C), F32), pltpu.VMEM((CELLS, C), F32)],
        2 * CELLS * 8 * C * C,
        (SMEM,),
    )
    state = exchange(states.reshape(32, 32, C), TM).reshape(SIDE, 2, FRAMES, C)
    first, second = call(
        norm_kernel,
        [struct((SIDE, FRAMES, C), BF16)] * 2,
        (state, gain_s, scaling, offset),
        [],
        10 * CELLS * C,
    )
    count = lax.axis_size("frame")
    left = lax.ppermute(second, "frame", [(k, k + 1) for k in range(count - 1)])
    right = lax.ppermute(first, "frame", [(k + 1, k) for k in range(count - 1)])
    (terms,) = call(
        second_kernel,
        [struct((FRAMES, 64, C), BF16)],
        (scalars, state, left, first, second, right, space_weight, gain_a, attention_weight, output_weight),
        [
            pltpu.VMEM((4, SIDE + 2, FRAMES, C), BF16),
            pltpu.VMEM((2, CELLS // 2, C), F32),
            pltpu.VMEM((128, C), F32),
            pltpu.VMEM((FRAMES, 64, C), F32),
        ],
        2 * CELLS * 17 * C * C,
        (SMEM,),
    )
    (terms,) = call(
        frame_kernel,
        [struct((CELLS, C), BF16)],
        (scalars, exchange(terms, "frame"), noise.reshape(CELLS, C)),
        [pltpu.VMEM((CELLS, C), F32)],
        2 * CELLS * C,
        (SMEM,),
    )
    terms = exchange(terms.reshape(32, 32, C), TM).reshape(CELLS, C)
    (sums,) = call(sum_kernel, [struct((CELLS, C), F32)], (terms,), [], 2 * CELLS * C)
    sums = exchange(sums.reshape(32, 32, C), TM).reshape(SIDE, SIDE, C)
    return (start + sums)[None, None]


def solution(mesh):
    finer = Mesh(mesh.devices.reshape(4, 8, mesh.shape["frame"]), ALL)
    placed = (
        P("frame", None, None, None),
        P(TM, "frame", None, None, None),
        P(TM, "frame", None, None, None),
        P(TM),
        P(),
        P(),
        P(),
        P(),
        P(),
        P(),
    )
    return jax.shard_map(
        shards,
        mesh=finer,
        in_specs=placed,
        out_specs=P(TM, "frame", None, None, None),
        check_vma=False,
    )
```

```python
import math

import jax
import jax.numpy as jnp
from jax import lax
from jax.experimental import pallas as pl
from jax.experimental.pallas import tpu as pltpu
from jax.sharding import Mesh
from jax.sharding import PartitionSpec as P

C = 128
HEAD_DIM = 64
FRAMES = 16
STEPS = 32
SIDE = 32
CELLS = SIDE * SIDE
TM = ("tm_0", "tm_1")
ALL = ("tm_0", "tm_1", "frame")
F32 = jnp.float32
BF16 = jnp.bfloat16
VMEM = pl.BlockSpec(memory_space=pltpu.VMEM)
SMEM = pl.BlockSpec(memory_space=pltpu.SMEM)
FAR = pl.BlockSpec(memory_space=pltpu.HBM)


def dot(left, right):
    return jnp.dot(left, right, preferred_element_type=F32)


def unit(field, gain):
    return field * lax.rsqrt(jnp.mean(field * field, axis=-1, keepdims=True) + 1e-06) * gain


def attention_masks(cell_major):
    row = lax.broadcasted_iota(jnp.int32, (128, 128), 0)
    lane = lax.broadcasted_iota(jnp.int32, (128, 128), 1)
    same_cell = row // FRAMES == lane // FRAMES if cell_major else row % 8 == lane % 8
    return same_cell, lane < HEAD_DIM


def attend_block(mixed, gain, attention_weight, output_weight, masks):
    same_cell, first_head = masks
    projected = dot(unit(mixed, gain).astype(BF16), attention_weight).astype(BF16)
    queries, keys, values = (projected[:, i * C : (i + 1) * C] for i in range(3))
    zero = jnp.zeros((), BF16)
    attended = None
    for head in range(2):
        lanes = first_head if head == 0 else jnp.logical_not(first_head)
        scores = lax.dot_general(
            jnp.where(lanes, queries, zero), keys, (((1,), (1,)), ((), ())), preferred_element_type=F32
        ) * (1.0 / math.sqrt(HEAD_DIM))
        scores = jnp.where(same_cell, scores, -1e30)
        grown = jnp.exp(scores - jnp.max(scores, axis=-1, keepdims=True))
        weights = (grown * (1.0 / jnp.sum(grown, axis=-1, keepdims=True))).astype(BF16)
        part = dot(weights, jnp.where(lanes, values, zero))
        attended = part if attended is None else attended + part
    return dot(attended.astype(BF16), output_weight)


def times(step):
    value = step[0].astype(F32) / 1000.0
    return value, (0.5 + value) / math.sqrt(STEPS)


def first_kernel(
    step, guess_far, noise_far, start_far, weight_far, map_far, encoded, gain_s, gain_a, out, params,
    guess, noise, start, space_weight, time_weight, padded, mixed, drawn, packed, sems,
):
    copies = [
        pltpu.make_async_copy(far, near, sems.at[i])
        for i, (far, near) in enumerate(
            (
                (guess_far, guess),
                (weight_far, space_weight),
                (noise_far, noise),
                (start_far, start),
                (map_far, time_weight),
            )
        )
    ]
    for copy in copies:
        copy.start()
    col = lax.broadcasted_iota(jnp.int32, (8, SIDE, C), 1)
    padded[0] = jnp.zeros((SIDE, 3 * C), BF16)
    padded[SIDE + 1] = jnp.zeros((SIDE, 3 * C), BF16)
    copies[4].wait()
    shifted = jnp.dot(
        jnp.broadcast_to(encoded[...], (8, C)), time_weight[...],
        precision=lax.Precision.HIGHEST, preferred_element_type=F32,
    )[0:1]
    scaling, offset = 1.0 + shifted[:, :C], shifted[:, C:]
    gain = gain_s[...]
    for i, row in enumerate((scaling, offset, gain, gain_a[...])):
        params[pl.ds(i * 16, 16), :] = jnp.broadcast_to(row, (16, C))
    copies[0].wait()
    for block in range(4):
        rows = pl.ds(block * 8, 8)
        state = guess[rows]
        normed = unit(state, gain) * scaling + offset
        left = jnp.where(col == 0, 0.0, pltpu.roll(normed, 1, 1))
        right = jnp.where(col == SIDE - 1, 0.0, pltpu.roll(normed, SIDE - 1, 1))
        at = pl.ds(block * 8 + 1, 8)
        padded[at, :, 0:C] = left.astype(BF16)
        padded[at, :, C : 2 * C] = normed.astype(BF16)
        padded[at, :, 2 * C : 3 * C] = right.astype(BF16)
    copies[1].wait()
    total = None
    for shift in range(3):
        part = dot(
            padded[shift : shift + SIDE].reshape(CELLS, 3 * C),
            space_weight[shift * 3 * C : (shift + 1) * 3 * C, :],
        )
        total = part if total is None else total + part
    mixed[...] = total
    copies[2].wait()
    copies[3].wait()
    time_value, coefficient = times(step)
    scale = time_value * coefficient
    last = lax.axis_index("tm_0") * lax.axis_size("tm_1") + lax.axis_index("tm_1") == STEPS - 1
    for block in range(8):
        rows = pl.ds(block * 128, 128)
        band = pl.ds(block * 4, 4)
        conv = mixed[rows, :]
        here = guess[band].reshape(128, C) + conv * jax.nn.sigmoid(conv)
        begun = start[band].reshape(128, C)
        begun_high = begun.astype(BF16).astype(F32)
        mixed[rows, :] = jnp.where(last, begun - begun_high, here)
        drawn[rows, :] = jnp.where(last, begun_high, noise[band].reshape(128, C) * scale)
    for block in range(8):
        half = CELLS // 16
        for slot, source in enumerate((mixed, mixed, drawn, drawn)):
            packed[pl.ds(block * 256 + slot, half, 4), :] = source[pl.ds(block * 128 + slot % 2, half, 2), :]
        rows = pl.ds(block * 256, 256)
        out[rows, :] = packed[rows, :].astype(BF16)


def owner_kernel(all_steps, received, params, attention_weight, output_weight, states, noise_before, wide, drifts):
    masks = attention_masks(True)
    wide[...] = received[...].astype(F32)
    for cell in range(2):
        for block in range(4):
            mixed = wide[pl.ds(block * 512 + cell, 128, 4), :]
            drifts[pl.ds(cell * 512 + block * 128, 128), :] = mixed + attend_block(
                mixed, params[48:49, :], attention_weight[...], output_weight[...], masks
            )
    for cell in range(2):
        tail = (STEPS - 1) * FRAMES * 4 + cell
        state = wide[pl.ds(tail + 2, FRAMES, 4), :] + wide[pl.ds(tail, FRAMES, 4), :]
        noises = jnp.zeros((FRAMES, C), F32)
        for step in range(STEPS):
            states[pl.ds(step * 32 + cell * FRAMES, FRAMES), :] = state.astype(BF16)
            noise_before[pl.ds(step * 32 + cell * FRAMES, FRAMES), :] = noises
            if step < STEPS - 1:
                drawn = wide[pl.ds(step * FRAMES * 4 + 2 + cell, FRAMES, 4), :]
                drift = drifts[pl.ds(cell * 512 + step * FRAMES, FRAMES), :]
                coefficient = (0.5 + all_steps[step].astype(F32) / 1000.0) / math.sqrt(STEPS)
                state = state + (coefficient * drift + drawn)
                noises = noises + drawn


def norm_kernel(state, params, first, second):
    for cell, out in ((0, first), (1, second)):
        for block in range(4):
            rows = state[pl.ds(block * 8, 8), cell].astype(F32)
            normed = unit(rows, params[32:33, :]) * params[0:1, :] + params[16:17, :]
            out[pl.ds(block * 8, 8)] = normed.astype(BF16)


def second_kernel(
    step, state, left, first, second, right, space_weight, params, attention_weight, output_weight, out, padded, conv
):
    for col, piece in enumerate((left, first, second, right)):
        padded[col, 0] = jnp.zeros((FRAMES, C), BF16)
        padded[col, SIDE + 1] = jnp.zeros((FRAMES, C), BF16)
        padded[col, 1 : SIDE + 1] = piece[...]
    for cell in range(2):
        taps = [
            padded[cell + across, down : down + SIDE].reshape(SIDE * FRAMES, C)
            for down in range(3)
            for across in range(3)
        ]
        conv[cell] = dot(jnp.concatenate(taps, axis=-1), space_weight[...])
    masks = attention_masks(True)
    coefficient = times(step)[1]
    for cell in range(2):
        for block in range(4):
            found = conv[cell, pl.ds(block * 128, 128), :]
            here = state[pl.ds(block * 8, 8), cell].reshape(128, C).astype(F32)
            mixed = here + found * jax.nn.sigmoid(found)
            drift = mixed + attend_block(
                mixed, params[48:49, :], attention_weight[...], output_weight[...], masks
            )
            out[pl.ds(block * 8, 8), cell] = (coefficient * drift).reshape(8, FRAMES, C).astype(BF16)


def sum_kernel(received, noise_before, out):
    for cell in range(2):
        total = jnp.zeros((FRAMES, C), F32)
        for step in range(STEPS):
            rows = pl.ds(step * 32 + cell * FRAMES, FRAMES)
            total = total + received[rows, :].astype(F32)
            out[pl.ds(step * 32 + cell, FRAMES, 2), :] = total + noise_before[rows, :]


def call(kernel, outs, operands, scratch, flops, spaces=(), grant=16):
    specs = [*spaces, *[VMEM] * (len(operands) - len(spaces))]
    moved = sum(x.size * x.dtype.itemsize for x in (*operands, *outs))
    return pl.pallas_call(
        kernel,
        out_shape=outs,
        in_specs=specs,
        out_specs=[VMEM] * len(outs),
        scratch_shapes=scratch,
        compiler_params=pltpu.CompilerParams(vmem_limit_bytes=grant << 20),
        cost_estimate=pl.CostEstimate(flops=flops, bytes_accessed=moved, transcendentals=0),
    )(*operands)


def struct(shape, dtype):
    return jax.ShapeDtypeStruct(shape, dtype)


def embed_time(step_value):
    half_width = C // 2
    lane = jnp.arange(C)
    frequency = jnp.exp(-math.log(10000.0) * (lane % half_width).astype(F32) / half_width)
    angles = step_value.astype(F32) * frequency
    return jnp.where(lane < half_width, jnp.cos(angles), jnp.sin(angles))[None, :]


def exchange(array, axes):
    return lax.all_to_all(array, axes, 0, 0, tiled=True)


def shards(
    start_state,
    initial_guess,
    noise_draws,
    timesteps,
    gain_space,
    gain_attention,
    time_weight,
    space_weight,
    attention_weight,
    output_weight,
):
    guess, noise, start = initial_guess[0, 0], noise_draws[0, 0], start_state[0]
    time_value = timesteps[0].astype(F32) / 1000.0
    own_scale = time_value * (0.5 + time_value) / math.sqrt(STEPS)
    encoded, own_scale = lax.optimization_barrier((embed_time(timesteps[0]), own_scale))
    sent, params = call(
        first_kernel,
        [struct((2 * CELLS, C), BF16), struct((64, C), F32)],
        (
            timesteps, guess, noise, start, space_weight, time_weight,
            encoded, gain_space[None, :], gain_attention[None, :],
        ),
        [
            pltpu.VMEM((SIDE, SIDE, C), F32),
            pltpu.VMEM((SIDE, SIDE, C), F32),
            pltpu.VMEM((SIDE, SIDE, C), F32),
            pltpu.VMEM((9 * C, C), BF16),
            pltpu.VMEM((C, 2 * C), F32),
            pltpu.VMEM((SIDE + 2, SIDE, 3 * C), BF16),
            pltpu.VMEM((CELLS, C), F32),
            pltpu.VMEM((CELLS, C), F32),
            pltpu.VMEM((2 * CELLS, C), F32),
            pltpu.SemaphoreType.DMA((5,)),
        ],
        2 * CELLS * 9 * C * C,
        (SMEM, FAR, FAR, FAR, FAR, FAR),
        62,
    )
    received = exchange(sent.reshape(512, 4, C), ALL).reshape(2 * CELLS, C)
    all_steps = lax.all_gather(timesteps, TM, tiled=True)
    states, noise_before = call(
        owner_kernel,
        [struct((CELLS, C), BF16), struct((CELLS, C), F32)],
        (all_steps, received, params, attention_weight, output_weight),
        [pltpu.VMEM((2 * CELLS, C), F32), pltpu.VMEM((CELLS, C), F32)],
        2 * CELLS * 8 * C * C,
        (SMEM,),
    )
    state = exchange(states.reshape(32, 32, C), TM).reshape(SIDE, 2, FRAMES, C)
    first, second = call(
        norm_kernel,
        [struct((SIDE, FRAMES, C), BF16)] * 2,
        (state, params),
        [],
        10 * CELLS * C,
    )
    count = lax.axis_size("frame")
    left = lax.ppermute(second, "frame", [(k, k + 1) for k in range(count - 1)])
    right = lax.ppermute(first, "frame", [(k + 1, k) for k in range(count - 1)])
    (drifts,) = call(
        second_kernel,
        [struct((SIDE, 2, FRAMES, C), BF16)],
        (timesteps, state, left, first, second, right, space_weight, params, attention_weight, output_weight),
        [pltpu.VMEM((4, SIDE + 2, FRAMES, C), BF16), pltpu.VMEM((2, CELLS // 2, C), F32)],
        2 * CELLS * 17 * C * C,
        (SMEM,),
    )
    drifts = exchange(drifts.reshape(32, 32, C), TM).reshape(CELLS, C)
    (sums,) = call(sum_kernel, [struct((CELLS, C), F32)], (drifts, noise_before), [], 2 * CELLS * C)
    sums = exchange(sums.reshape(512, 2, C), ALL).reshape(SIDE, SIDE, C)
    return (start + (sums + own_scale * noise))[None, None]


def solution(mesh):
    finer = Mesh(mesh.devices.reshape(4, 8, mesh.shape["frame"]), ALL)
    placed = (
        P("frame", None, None, None),
        P(TM, "frame", None, None, None),
        P(TM, "frame", None, None, None),
        P(TM),
        P(),
        P(),
        P(),
        P(),
        P(),
        P(),
    )
    return jax.shard_map(
        shards,
        mesh=finer,
        in_specs=placed,
        out_specs=P(TM, "frame", None, None, None),
        check_vma=False,
    )
```

```python
import math

import jax
import jax.numpy as jnp
from jax import lax
from jax.experimental import pallas as pl
from jax.experimental.pallas import tpu as pltpu
from jax.sharding import Mesh
from jax.sharding import PartitionSpec as P

C = 128
HEAD_DIM = 64
FRAMES = 16
STEPS = 32
SIDE = 32
CELLS = SIDE * SIDE
TM = ("tm_0", "tm_1")
ALL = ("tm_0", "tm_1", "frame")
F32 = jnp.float32
BF16 = jnp.bfloat16
VMEM = pl.BlockSpec(memory_space=pltpu.VMEM)
SMEM = pl.BlockSpec(memory_space=pltpu.SMEM)
FAR = pl.BlockSpec(memory_space=pltpu.HBM)


def dot(left, right):
    return jnp.dot(left, right, preferred_element_type=F32)


def unit(field, gain):
    return field * lax.rsqrt(jnp.mean(field * field, axis=-1, keepdims=True) + 1e-06) * gain


def attend(load, emit, gain, attention_weight, output_weight, normed, query_key, values_t, attended_t):
    row = lax.broadcasted_iota(jnp.int32, (128, 128), 0)
    lane = lax.broadcasted_iota(jnp.int32, (128, 128), 1)
    first_head = lane < HEAD_DIM
    same_cell = row // FRAMES == lane // FRAMES
    zero = jnp.zeros((), BF16)
    for block in range(8):
        normed[pl.ds(block * 128, 128), :] = unit(load(block), gain).astype(BF16)
    query_key[...] = dot(normed[...], attention_weight[:, 0 : 2 * C]).astype(BF16)
    values_t[...] = lax.dot_general(
        attention_weight[:, 2 * C :].T, normed[...], (((1,), (1,)), ((), ())), preferred_element_type=F32
    ).astype(BF16)
    for block in range(8):
        rows = pl.ds(block * 128, 128)
        keys = query_key[rows, C : 2 * C]
        keys = jnp.concatenate(
            [jnp.where(first_head, keys, zero), jnp.where(first_head, zero, keys)], axis=0
        )
        scores_t = lax.dot_general(
            keys, query_key[rows, 0:C], (((1,), (1,)), ((), ())), preferred_element_type=F32
        )
        parts = []
        for head in range(2):
            kept = jnp.where(same_cell, scores_t[head * 128 : (head + 1) * 128], 0.0)
            scores = jnp.sum(kept.reshape(8, FRAMES, 128), axis=0) * (1.0 / math.sqrt(HEAD_DIM))
            grown = jnp.exp(scores - jnp.max(scores, axis=0, keepdims=True))
            weights = grown * (1.0 / jnp.sum(grown, axis=0, keepdims=True))
            spread = jnp.where(same_cell, jnp.concatenate([weights] * 8, axis=0), 0.0)
            held = values_t[head * HEAD_DIM : (head + 1) * HEAD_DIM, rows]
            parts.append(dot(held, spread.astype(BF16)))
        attended_t[:, rows] = jnp.concatenate(parts, axis=0).astype(BF16)
    for block in range(8):
        emit(
            block,
            lax.dot_general(
                attended_t[:, pl.ds(block * 128, 128)],
                output_weight[...],
                (((0,), (0,)), ((), ())),
                preferred_element_type=F32,
            ),
        )


def times(step):
    value = step[0].astype(F32) / 1000.0
    return value, (0.5 + value) / math.sqrt(STEPS)


def first_kernel(
    step, guess_far, noise_far, start_far, weight_far, map_far, encoded, gain_s, gain_a, out, params,
    guess, noise, start, space_weight, time_weight, padded, mixed, drawn, packed, sems,
):
    copies = [
        pltpu.make_async_copy(far, near, sems.at[i])
        for i, (far, near) in enumerate(
            (
                (guess_far, guess),
                (weight_far, space_weight),
                (noise_far, noise),
                (start_far, start),
                (map_far, time_weight),
            )
        )
    ]
    for copy in copies:
        copy.start()
    col = lax.broadcasted_iota(jnp.int32, (8, SIDE, C), 1)
    padded[0] = jnp.zeros((SIDE, 3 * C), BF16)
    padded[SIDE + 1] = jnp.zeros((SIDE, 3 * C), BF16)
    copies[4].wait()
    shifted = jnp.dot(
        jnp.broadcast_to(encoded[...], (8, C)), time_weight[...],
        precision=lax.Precision.HIGHEST, preferred_element_type=F32,
    )[0:1]
    scaling, offset = 1.0 + shifted[:, :C], shifted[:, C:]
    gain = gain_s[...]
    for i, row in enumerate((scaling, offset, gain, gain_a[...])):
        params[pl.ds(i * 16, 16), :] = jnp.broadcast_to(row, (16, C))
    copies[0].wait()
    for block in range(4):
        rows = pl.ds(block * 8, 8)
        state = guess[rows]
        normed = unit(state, gain) * scaling + offset
        left = jnp.where(col == 0, 0.0, pltpu.roll(normed, 1, 1))
        right = jnp.where(col == SIDE - 1, 0.0, pltpu.roll(normed, SIDE - 1, 1))
        at = pl.ds(block * 8 + 1, 8)
        padded[at, :, 0:C] = left.astype(BF16)
        padded[at, :, C : 2 * C] = normed.astype(BF16)
        padded[at, :, 2 * C : 3 * C] = right.astype(BF16)
    copies[1].wait()
    total = None
    for shift in range(3):
        part = dot(
            padded[shift : shift + SIDE].reshape(CELLS, 3 * C),
            space_weight[shift * 3 * C : (shift + 1) * 3 * C, :],
        )
        total = part if total is None else total + part
    mixed[...] = total
    copies[2].wait()
    copies[3].wait()
    time_value, coefficient = times(step)
    scale = time_value * coefficient
    last = lax.axis_index("tm_0") * lax.axis_size("tm_1") + lax.axis_index("tm_1") == STEPS - 1
    for block in range(8):
        rows = pl.ds(block * 128, 128)
        band = pl.ds(block * 4, 4)
        conv = mixed[rows, :]
        here = guess[band].reshape(128, C) + conv * jax.nn.sigmoid(conv)
        begun = start[band].reshape(128, C)
        begun_high = begun.astype(BF16).astype(F32)
        mixed[rows, :] = jnp.where(last, begun - begun_high, here)
        drawn[rows, :] = jnp.where(last, begun_high, noise[band].reshape(128, C) * scale)
    for block in range(8):
        half = CELLS // 16
        for slot, source in enumerate((mixed, mixed, drawn, drawn)):
            packed[pl.ds(block * 256 + slot, half, 4), :] = source[pl.ds(block * 128 + slot % 2, half, 2), :]
        rows = pl.ds(block * 256, 256)
        out[rows, :] = packed[rows, :].astype(BF16)


def owner_kernel(
    all_steps, received, params, attention_weight, output_weight, states, noise_before,
    wide, drifts, *room,
):
    wide[...] = received[...].astype(F32)

    def load(block):
        return wide[pl.ds(block % 4 * 512 + block // 4, 128, 4), :]

    def emit(block, found):
        drifts[pl.ds(block * 128, 128), :] = load(block) + found

    attend(load, emit, params[48:49, :], attention_weight, output_weight, *room)
    for cell in range(2):
        tail = (STEPS - 1) * FRAMES * 4 + cell
        state = wide[pl.ds(tail + 2, FRAMES, 4), :] + wide[pl.ds(tail, FRAMES, 4), :]
        noises = jnp.zeros((FRAMES, C), F32)
        for step in range(STEPS):
            states[pl.ds(step * 32 + cell * FRAMES, FRAMES), :] = state.astype(BF16)
            noise_before[pl.ds(step * 32 + cell * FRAMES, FRAMES), :] = noises
            if step < STEPS - 1:
                drawn = wide[pl.ds(step * FRAMES * 4 + 2 + cell, FRAMES, 4), :]
                drift = drifts[pl.ds(cell * 512 + step * FRAMES, FRAMES), :]
                coefficient = (0.5 + all_steps[step].astype(F32) / 1000.0) / math.sqrt(STEPS)
                state = state + (coefficient * drift + drawn)
                noises = noises + drawn


def norm_kernel(state, params, first, second):
    for cell, out in ((0, first), (1, second)):
        for block in range(4):
            rows = state[pl.ds(block * 8, 8), cell].astype(F32)
            normed = unit(rows, params[32:33, :]) * params[0:1, :] + params[16:17, :]
            out[pl.ds(block * 8, 8)] = normed.astype(BF16)


def second_kernel(
    step, state, left, first, second, right, space_weight, params, attention_weight, output_weight,
    out, padded, mixed, *room,
):
    for col, piece in enumerate((left, first, second, right)):
        padded[col, 0] = jnp.zeros((FRAMES, C), BF16)
        padded[col, SIDE + 1] = jnp.zeros((FRAMES, C), BF16)
        padded[col, 1 : SIDE + 1] = piece[...]
    for cell in range(2):
        taps = [
            padded[cell + across, down : down + SIDE].reshape(SIDE * FRAMES, C)
            for down in range(3)
            for across in range(3)
        ]
        mixed[pl.ds(cell * 512, 512), :] = dot(jnp.concatenate(taps, axis=-1), space_weight[...])
    coefficient = times(step)[1]
    for block in range(8):
        rows = pl.ds(block * 128, 128)
        found = mixed[rows, :]
        here = state[pl.ds(block % 4 * 8, 8), block // 4].reshape(128, C).astype(F32)
        mixed[rows, :] = here + found * jax.nn.sigmoid(found)

    def load(block):
        return mixed[pl.ds(block * 128, 128), :]

    def emit(block, found):
        drift = coefficient * (load(block) + found)
        out[pl.ds(block % 4 * 8, 8), block // 4] = drift.reshape(8, FRAMES, C).astype(BF16)

    attend(load, emit, params[48:49, :], attention_weight, output_weight, *room)


def sum_kernel(received, noise_before, out):
    for cell in range(2):
        total = jnp.zeros((FRAMES, C), F32)
        for step in range(STEPS):
            rows = pl.ds(step * 32 + cell * FRAMES, FRAMES)
            total = total + received[rows, :].astype(F32)
            out[pl.ds(step * 32 + cell, FRAMES, 2), :] = total + noise_before[rows, :]


def call(kernel, outs, operands, scratch, flops, spaces=(), grant=16):
    specs = [*spaces, *[VMEM] * (len(operands) - len(spaces))]
    moved = sum(x.size * x.dtype.itemsize for x in (*operands, *outs))
    return pl.pallas_call(
        kernel,
        out_shape=outs,
        in_specs=specs,
        out_specs=[VMEM] * len(outs),
        scratch_shapes=scratch,
        compiler_params=pltpu.CompilerParams(vmem_limit_bytes=grant << 20),
        cost_estimate=pl.CostEstimate(flops=flops, bytes_accessed=moved, transcendentals=0),
    )(*operands)


def attention_room():
    return [
        pltpu.VMEM((CELLS, C), BF16),
        pltpu.VMEM((CELLS, 2 * C), BF16),
        pltpu.VMEM((C, CELLS), BF16),
        pltpu.VMEM((C, CELLS), BF16),
    ]


def struct(shape, dtype):
    return jax.ShapeDtypeStruct(shape, dtype)


def embed_time(step_value):
    half_width = C // 2
    lane = jnp.arange(C)
    frequency = jnp.exp(-math.log(10000.0) * (lane % half_width).astype(F32) / half_width)
    angles = step_value.astype(F32) * frequency
    return jnp.where(lane < half_width, jnp.cos(angles), jnp.sin(angles))[None, :]


def exchange(array, axes):
    return lax.all_to_all(array, axes, 0, 0, tiled=True)


def shards(
    start_state,
    initial_guess,
    noise_draws,
    timesteps,
    gain_space,
    gain_attention,
    time_weight,
    space_weight,
    attention_weight,
    output_weight,
):
    guess, noise, start = initial_guess[0, 0], noise_draws[0, 0], start_state[0]
    time_value = timesteps[0].astype(F32) / 1000.0
    own_scale = time_value * (0.5 + time_value) / math.sqrt(STEPS)
    encoded, own_scale = lax.optimization_barrier((embed_time(timesteps[0]), own_scale))
    sent, params = call(
        first_kernel,
        [struct((2 * CELLS, C), BF16), struct((64, C), F32)],
        (
            timesteps, guess, noise, start, space_weight, time_weight,
            encoded, gain_space[None, :], gain_attention[None, :],
        ),
        [
            pltpu.VMEM((SIDE, SIDE, C), F32),
            pltpu.VMEM((SIDE, SIDE, C), F32),
            pltpu.VMEM((SIDE, SIDE, C), F32),
            pltpu.VMEM((9 * C, C), BF16),
            pltpu.VMEM((C, 2 * C), F32),
            pltpu.VMEM((SIDE + 2, SIDE, 3 * C), BF16),
            pltpu.VMEM((CELLS, C), F32),
            pltpu.VMEM((CELLS, C), F32),
            pltpu.VMEM((2 * CELLS, C), F32),
            pltpu.SemaphoreType.DMA((5,)),
        ],
        2 * CELLS * 9 * C * C,
        (SMEM, FAR, FAR, FAR, FAR, FAR),
        62,
    )
    received = exchange(sent.reshape(512, 4, C), ALL).reshape(2 * CELLS, C)
    all_steps = lax.all_gather(timesteps, TM, tiled=True)
    states, noise_before = call(
        owner_kernel,
        [struct((CELLS, C), BF16), struct((CELLS, C), F32)],
        (all_steps, received, params, attention_weight, output_weight),
        [pltpu.VMEM((2 * CELLS, C), F32), pltpu.VMEM((CELLS, C), F32), *attention_room()],
        2 * CELLS * 8 * C * C,
        (SMEM,),
    )
    state = exchange(states.reshape(32, 32, C), TM).reshape(SIDE, 2, FRAMES, C)
    first, second = call(
        norm_kernel,
        [struct((SIDE, FRAMES, C), BF16)] * 2,
        (state, params),
        [],
        10 * CELLS * C,
    )
    count = lax.axis_size("frame")
    left = lax.ppermute(second, "frame", [(k, k + 1) for k in range(count - 1)])
    right = lax.ppermute(first, "frame", [(k + 1, k) for k in range(count - 1)])
    (drifts,) = call(
        second_kernel,
        [struct((SIDE, 2, FRAMES, C), BF16)],
        (
            timesteps, state, left, first, second, right, space_weight, params,
            attention_weight, output_weight,
        ),
        [pltpu.VMEM((4, SIDE + 2, FRAMES, C), BF16), pltpu.VMEM((CELLS, C), F32), *attention_room()],
        2 * CELLS * 17 * C * C,
        (SMEM,),
    )
    drifts = exchange(drifts.reshape(32, 32, C), TM).reshape(CELLS, C)
    (sums,) = call(sum_kernel, [struct((CELLS, C), F32)], (drifts, noise_before), [], 2 * CELLS * C)
    sums = exchange(sums.reshape(512, 2, C), ALL).reshape(SIDE, SIDE, C)
    return (start + (sums + own_scale * noise))[None, None]


def solution(mesh):
    finer = Mesh(mesh.devices.reshape(4, 8, mesh.shape["frame"]), ALL)
    placed = (
        P("frame", None, None, None),
        P(TM, "frame", None, None, None),
        P(TM, "frame", None, None, None),
        P(TM),
        P(),
        P(),
        P(),
        P(),
        P(),
        P(),
    )
    return jax.shard_map(
        shards,
        mesh=finer,
        in_specs=placed,
        out_specs=P(TM, "frame", None, None, None),
        check_vma=False,
    )
```

```python
import math

import jax
import jax.numpy as jnp
from jax import lax
from jax.experimental import pallas as pl
from jax.experimental.pallas import tpu as pltpu
from jax.sharding import Mesh
from jax.sharding import PartitionSpec as P

C = 128
HEAD_DIM = 64
FRAMES = 16
STEPS = 32
SIDE = 32
CELLS = SIDE * SIDE
TM = ("tm_0", "tm_1")
ALL = ("tm_0", "tm_1", "frame")
F32 = jnp.float32
BF16 = jnp.bfloat16
VMEM = pl.BlockSpec(memory_space=pltpu.VMEM)
SMEM = pl.BlockSpec(memory_space=pltpu.SMEM)
FAR = pl.BlockSpec(memory_space=pltpu.HBM)


def dot(left, right):
    return jnp.dot(left, right, preferred_element_type=F32)


def unit(field, gain):
    return field * lax.rsqrt(jnp.mean(field * field, axis=-1, keepdims=True) + 1e-06) * gain


def attend(load, emit, gain, attention_weight, output_weight, normed, query_key, values_t, attended_t):
    row = lax.broadcasted_iota(jnp.int32, (128, 128), 0)
    lane = lax.broadcasted_iota(jnp.int32, (128, 128), 1)
    first_head = lane < HEAD_DIM
    same_cell = row // FRAMES == lane // FRAMES
    zero = jnp.zeros((), BF16)
    for block in range(8):
        normed[pl.ds(block * 128, 128), :] = unit(load(block), gain).astype(BF16)
    query_key[...] = dot(normed[...], attention_weight[:, 0 : 2 * C]).astype(BF16)
    values_t[...] = lax.dot_general(
        attention_weight[:, 2 * C :].T, normed[...], (((1,), (1,)), ((), ())), preferred_element_type=F32
    ).astype(BF16)
    for block in range(8):
        rows = pl.ds(block * 128, 128)
        keys = query_key[rows, C : 2 * C]
        keys = jnp.concatenate(
            [jnp.where(first_head, keys, zero), jnp.where(first_head, zero, keys)], axis=0
        )
        scores_t = lax.dot_general(
            keys, query_key[rows, 0:C], (((1,), (1,)), ((), ())), preferred_element_type=F32
        )
        parts = []
        for head in range(2):
            kept = jnp.where(same_cell, scores_t[head * 128 : (head + 1) * 128], 0.0)
            scores = jnp.sum(kept.reshape(8, FRAMES, 128), axis=0) * (1.0 / math.sqrt(HEAD_DIM))
            grown = jnp.exp(scores - jnp.max(scores, axis=0, keepdims=True))
            weights = grown * (1.0 / jnp.sum(grown, axis=0, keepdims=True))
            spread = jnp.where(same_cell, jnp.concatenate([weights] * 8, axis=0), 0.0)
            held = values_t[head * HEAD_DIM : (head + 1) * HEAD_DIM, rows]
            parts.append(dot(held, spread.astype(BF16)))
        attended_t[:, rows] = jnp.concatenate(parts, axis=0).astype(BF16)
    for block in range(8):
        emit(
            block,
            lax.dot_general(
                attended_t[:, pl.ds(block * 128, 128)],
                output_weight[...],
                (((0,), (0,)), ((), ())),
                preferred_element_type=F32,
            ),
        )


def times(step):
    value = step[0].astype(F32) / 1000.0
    return value, (0.5 + value) / math.sqrt(STEPS)


def first_kernel(
    step, guess_far, noise_far, start_far, weight_far, map_far, gain_s, gain_a, out, params,
    guess, noise, start, space_weight, time_weight, padded, mixed, drawn, packed, sems,
):
    copies = [
        pltpu.make_async_copy(far, near, sems.at[i])
        for i, (far, near) in enumerate(
            (
                (map_far, time_weight),
                (guess_far, guess),
                (weight_far, space_weight),
                (noise_far, noise),
                (start_far, start),
            )
        )
    ]
    for copy in copies:
        copy.start()
    col = lax.broadcasted_iota(jnp.int32, (8, SIDE, C), 1)
    padded[0] = jnp.zeros((SIDE, 3 * C), BF16)
    padded[SIDE + 1] = jnp.zeros((SIDE, 3 * C), BF16)
    copies[0].wait()
    lane = lax.broadcasted_iota(jnp.int32, (8, C), 1)
    frequency = jnp.exp((lane % HEAD_DIM).astype(F32) * (-math.log(10000.0) / HEAD_DIM))
    angles = step[0].astype(F32) * frequency
    shifted = jnp.dot(
        jnp.where(lane < HEAD_DIM, jnp.cos(angles), jnp.sin(angles)), time_weight[...],
        precision=lax.Precision.HIGHEST, preferred_element_type=F32,
    )[0:1]
    scaling, offset = 1.0 + shifted[:, :C], shifted[:, C:]
    gain = gain_s[...]
    for i, row in enumerate((scaling, offset, gain, gain_a[...])):
        params[pl.ds(i * 16, 16), :] = jnp.broadcast_to(row, (16, C))
    copies[1].wait()
    for block in range(4):
        rows = pl.ds(block * 8, 8)
        state = guess[rows]
        normed = unit(state, gain) * scaling + offset
        left = jnp.where(col == 0, 0.0, pltpu.roll(normed, 1, 1))
        right = jnp.where(col == SIDE - 1, 0.0, pltpu.roll(normed, SIDE - 1, 1))
        at = pl.ds(block * 8 + 1, 8)
        padded[at, :, 0:C] = left.astype(BF16)
        padded[at, :, C : 2 * C] = normed.astype(BF16)
        padded[at, :, 2 * C : 3 * C] = right.astype(BF16)
    for copy in copies[2:]:
        copy.wait()
    total = None
    for shift in range(3):
        part = dot(
            padded[shift : shift + SIDE].reshape(CELLS, 3 * C),
            space_weight[shift * 3 * C : (shift + 1) * 3 * C, :],
        )
        total = part if total is None else total + part
    mixed[...] = total
    time_value, coefficient = times(step)
    scale = time_value * coefficient
    last = lax.axis_index("tm_0") * lax.axis_size("tm_1") + lax.axis_index("tm_1") == STEPS - 1
    for block in range(8):
        rows = pl.ds(block * 128, 128)
        band = pl.ds(block * 4, 4)
        conv = mixed[rows, :]
        here = guess[band].reshape(128, C) + conv * jax.nn.sigmoid(conv)
        begun = start[band].reshape(128, C)
        begun_high = begun.astype(BF16).astype(F32)
        mixed[rows, :] = jnp.where(last, begun - begun_high, here)
        drawn[rows, :] = jnp.where(last, begun_high, noise[band].reshape(128, C) * scale)
    for block in range(8):
        half = CELLS // 16
        for slot, source in enumerate((mixed, mixed, drawn, drawn)):
            packed[pl.ds(block * 256 + slot, half, 4), :] = source[pl.ds(block * 128 + slot % 2, half, 2), :]
        rows = pl.ds(block * 256, 256)
        out[rows, :] = packed[rows, :].astype(BF16)


def owner_kernel(
    all_steps, received, params, attention_weight, output_weight, states, noise_before,
    wide, drifts, *room,
):
    wide[...] = received[...].astype(F32)

    def load(block):
        return wide[pl.ds(block % 4 * 512 + block // 4, 128, 4), :]

    def emit(block, found):
        drifts[pl.ds(block * 128, 128), :] = load(block) + found

    attend(load, emit, params[48:49, :], attention_weight, output_weight, *room)
    for cell in range(2):
        tail = (STEPS - 1) * FRAMES * 4 + cell
        state = wide[pl.ds(tail + 2, FRAMES, 4), :] + wide[pl.ds(tail, FRAMES, 4), :]
        noises = jnp.zeros((FRAMES, C), F32)
        for step in range(STEPS):
            states[pl.ds(step * 32 + cell * FRAMES, FRAMES), :] = state.astype(BF16)
            noise_before[pl.ds(step * 32 + cell * FRAMES, FRAMES), :] = noises
            if step < STEPS - 1:
                drawn = wide[pl.ds(step * FRAMES * 4 + 2 + cell, FRAMES, 4), :]
                drift = drifts[pl.ds(cell * 512 + step * FRAMES, FRAMES), :]
                coefficient = (0.5 + all_steps[step].astype(F32) / 1000.0) / math.sqrt(STEPS)
                state = state + (coefficient * drift + drawn)
                noises = noises + drawn


def norm_kernel(state, params, inner, outer):
    odd = lax.axis_index("frame") % 2 == 1
    for block in range(4):
        rows = pl.ds(block * 8, 8)
        pair = [
            unit(state[rows, cell].astype(F32), params[32:33, :]) * params[0:1, :] + params[16:17, :]
            for cell in range(2)
        ]
        inner[rows] = jnp.where(odd, pair[0], pair[1]).astype(BF16)
        outer[rows] = jnp.where(odd, pair[1], pair[0]).astype(BF16)


def second_kernel(
    step, state, inner, outer, from_core, from_chip, space_weight, params, attention_weight, output_weight,
    out, padded, mixed, *room,
):
    odd = lax.axis_index("frame") % 2 == 1
    columns = ((from_chip, from_core), (outer, inner), (inner, outer), (from_core, from_chip))
    for col, (when_even, when_odd) in enumerate(columns):
        padded[col, 0] = jnp.zeros((FRAMES, C), BF16)
        padded[col, SIDE + 1] = jnp.zeros((FRAMES, C), BF16)

        @pl.when(odd)
        def _(col=col, piece=when_odd):
            padded[col, 1 : SIDE + 1] = piece[...]

        @pl.when(jnp.logical_not(odd))
        def _(col=col, piece=when_even):
            padded[col, 1 : SIDE + 1] = piece[...]

    for cell in range(2):
        taps = [
            padded[cell + across, down : down + SIDE].reshape(SIDE * FRAMES, C)
            for down in range(3)
            for across in range(3)
        ]
        mixed[pl.ds(cell * 512, 512), :] = dot(jnp.concatenate(taps, axis=-1), space_weight[...])
    coefficient = times(step)[1]
    for block in range(8):
        rows = pl.ds(block * 128, 128)
        found = mixed[rows, :]
        here = state[pl.ds(block % 4 * 8, 8), block // 4].reshape(128, C).astype(F32)
        mixed[rows, :] = here + found * jax.nn.sigmoid(found)

    def load(block):
        return mixed[pl.ds(block * 128, 128), :]

    def emit(block, found):
        drift = coefficient * (load(block) + found)
        out[pl.ds(block % 4 * 8, 8), block // 4] = drift.reshape(8, FRAMES, C).astype(BF16)

    attend(load, emit, params[48:49, :], attention_weight, output_weight, *room)


def sum_kernel(received, noise_before, out):
    for cell in range(2):
        total = jnp.zeros((FRAMES, C), F32)
        for step in range(STEPS):
            rows = pl.ds(step * 32 + cell * FRAMES, FRAMES)
            total = total + received[rows, :].astype(F32)
            out[pl.ds(step * 32 + cell, FRAMES, 2), :] = total + noise_before[rows, :]


def call(kernel, outs, operands, scratch, flops, spaces=(), grant=16):
    specs = [*spaces, *[VMEM] * (len(operands) - len(spaces))]
    moved = sum(x.size * x.dtype.itemsize for x in (*operands, *outs))
    return pl.pallas_call(
        kernel,
        out_shape=outs,
        in_specs=specs,
        out_specs=[VMEM] * len(outs),
        scratch_shapes=scratch,
        compiler_params=pltpu.CompilerParams(vmem_limit_bytes=grant << 20),
        cost_estimate=pl.CostEstimate(flops=flops, bytes_accessed=moved, transcendentals=0),
    )(*operands)


def attention_room():
    return [
        pltpu.VMEM((CELLS, C), BF16),
        pltpu.VMEM((CELLS, 2 * C), BF16),
        pltpu.VMEM((C, CELLS), BF16),
        pltpu.VMEM((C, CELLS), BF16),
    ]


def struct(shape, dtype):
    return jax.ShapeDtypeStruct(shape, dtype)


def exchange(array, axes):
    return lax.all_to_all(array, axes, 0, 0, tiled=True)


def shards(
    start_state,
    initial_guess,
    noise_draws,
    timesteps,
    gain_space,
    gain_attention,
    time_weight,
    space_weight,
    attention_weight,
    output_weight,
):
    guess, noise, start = initial_guess[0, 0], noise_draws[0, 0], start_state[0]
    time_value = timesteps[0].astype(F32) / 1000.0
    own_scale = time_value * (0.5 + time_value) / math.sqrt(STEPS)
    gain_space, own_scale = lax.optimization_barrier((gain_space, own_scale))
    sent, params = call(
        first_kernel,
        [struct((2 * CELLS, C), BF16), struct((64, C), F32)],
        (
            timesteps, guess, noise, start, space_weight, time_weight,
            gain_space[None, :], gain_attention[None, :],
        ),
        [
            pltpu.VMEM((SIDE, SIDE, C), F32),
            pltpu.VMEM((SIDE, SIDE, C), F32),
            pltpu.VMEM((SIDE, SIDE, C), F32),
            pltpu.VMEM((9 * C, C), BF16),
            pltpu.VMEM((C, 2 * C), F32),
            pltpu.VMEM((SIDE + 2, SIDE, 3 * C), BF16),
            pltpu.VMEM((CELLS, C), F32),
            pltpu.VMEM((CELLS, C), F32),
            pltpu.VMEM((2 * CELLS, C), F32),
            pltpu.SemaphoreType.DMA((5,)),
        ],
        2 * CELLS * 9 * C * C,
        (SMEM, FAR, FAR, FAR, FAR, FAR),
        62,
    )
    received = exchange(sent.reshape(512, 4, C), ALL).reshape(2 * CELLS, C)
    all_steps = lax.all_gather(timesteps, TM, tiled=True)
    states, noise_before = call(
        owner_kernel,
        [struct((CELLS, C), BF16), struct((CELLS, C), F32)],
        (all_steps, received, params, attention_weight, output_weight),
        [pltpu.VMEM((2 * CELLS, C), F32), pltpu.VMEM((CELLS, C), F32), *attention_room()],
        2 * CELLS * 8 * C * C,
        (SMEM,),
    )
    state = exchange(states.reshape(32, 32, C), TM).reshape(SIDE, 2, FRAMES, C)
    inner, outer = call(
        norm_kernel,
        [struct((SIDE, FRAMES, C), BF16)] * 2,
        (state, params),
        [],
        10 * CELLS * C,
    )
    count = lax.axis_size("frame")
    chips = [(k + i, k + 1 - i) for k in range(1, count - 1, 2) for i in range(2)]
    cores = [(k, k ^ 1) for k in range(count)]
    from_chip = lax.ppermute(outer, "frame", chips)
    from_core = lax.ppermute(inner, "frame", cores)
    (drifts,) = call(
        second_kernel,
        [struct((SIDE, 2, FRAMES, C), BF16)],
        (
            timesteps, state, inner, outer, from_core, from_chip, space_weight, params,
            attention_weight, output_weight,
        ),
        [pltpu.VMEM((4, SIDE + 2, FRAMES, C), BF16), pltpu.VMEM((CELLS, C), F32), *attention_room()],
        2 * CELLS * 17 * C * C,
        (SMEM,),
    )
    drifts = exchange(drifts.reshape(32, 32, C), TM).reshape(CELLS, C)
    (sums,) = call(sum_kernel, [struct((CELLS, C), F32)], (drifts, noise_before), [], 2 * CELLS * C)
    sums = exchange(sums.reshape(512, 2, C), ALL).reshape(SIDE, SIDE, C)
    return (start + (sums + own_scale * noise))[None, None]


def solution(mesh):
    finer = Mesh(mesh.devices.reshape(4, 8, mesh.shape["frame"]), ALL)
    placed = (
        P("frame", None, None, None),
        P(TM, "frame", None, None, None),
        P(TM, "frame", None, None, None),
        P(TM),
        P(),
        P(),
        P(),
        P(),
        P(),
        P(),
    )
    return jax.shard_map(
        shards,
        mesh=finer,
        in_specs=placed,
        out_specs=P(TM, "frame", None, None, None),
        check_vma=False,
    )
```

```python
import math

import jax
import jax.numpy as jnp
from jax import lax
from jax.experimental import pallas as pl
from jax.experimental.pallas import tpu as pltpu
from jax.sharding import Mesh
from jax.sharding import PartitionSpec as P

C = 128
HEAD_DIM = 64
FRAMES = 16
STEPS = 32
SIDE = 32
CELLS = SIDE * SIDE
TM = ("tm_0", "tm_1")
ALL = ("tm_0", "tm_1", "frame")
F32 = jnp.float32
BF16 = jnp.bfloat16
VMEM = pl.BlockSpec(memory_space=pltpu.VMEM)
SMEM = pl.BlockSpec(memory_space=pltpu.SMEM)
FAR = pl.BlockSpec(memory_space=pltpu.HBM)


def dot(left, right):
    return jnp.dot(left, right, preferred_element_type=F32)


def unit(field, gain):
    return field * lax.rsqrt(jnp.mean(field * field, axis=-1, keepdims=True) + 1e-06) * gain


def attend(load, emit, gain, attention_weight, output_weight, normed, query_key, values_t, attended_t):
    row = lax.broadcasted_iota(jnp.int32, (128, 128), 0)
    lane = lax.broadcasted_iota(jnp.int32, (128, 128), 1)
    first_head = lane < HEAD_DIM
    same_cell = row // FRAMES == lane // FRAMES
    zero = jnp.zeros((), BF16)
    for block in range(8):
        normed[pl.ds(block * 128, 128), :] = unit(load(block), gain).astype(BF16)
    query_key[...] = dot(normed[...], attention_weight[:, 0 : 2 * C]).astype(BF16)
    values_t[...] = lax.dot_general(
        attention_weight[:, 2 * C :].T, normed[...], (((1,), (1,)), ((), ())), preferred_element_type=F32
    ).astype(BF16)
    for block in range(8):
        rows = pl.ds(block * 128, 128)
        keys = query_key[rows, C : 2 * C]
        keys = jnp.concatenate(
            [jnp.where(first_head, keys, zero), jnp.where(first_head, zero, keys)], axis=0
        )
        scores_t = lax.dot_general(
            keys, query_key[rows, 0:C], (((1,), (1,)), ((), ())), preferred_element_type=F32
        )
        parts = []
        for head in range(2):
            kept = jnp.where(same_cell, scores_t[head * 128 : (head + 1) * 128], 0.0)
            scores = jnp.sum(kept.reshape(8, FRAMES, 128), axis=0) * (1.0 / math.sqrt(HEAD_DIM))
            grown = jnp.exp(scores - jnp.max(scores, axis=0, keepdims=True))
            weights = grown * (1.0 / jnp.sum(grown, axis=0, keepdims=True))
            spread = jnp.where(same_cell, jnp.concatenate([weights] * 8, axis=0), 0.0)
            held = values_t[head * HEAD_DIM : (head + 1) * HEAD_DIM, rows]
            parts.append(dot(held, spread.astype(BF16)))
        attended_t[:, rows] = jnp.concatenate(parts, axis=0).astype(BF16)
    for block in range(8):
        emit(
            block,
            lax.dot_general(
                attended_t[:, pl.ds(block * 128, 128)],
                output_weight[...],
                (((0,), (0,)), ((), ())),
                preferred_element_type=F32,
            ),
        )


def times(step):
    value = step[0].astype(F32) / 1000.0
    return value, (0.5 + value) / math.sqrt(STEPS)


def first_kernel(
    step, guess_far, noise_far, start_far, weight_far, map_far, gain_s, gain_a, out, params,
    guess, noise, start, space_weight, time_weight, padded, mixed, drawn, packed, sems,
):
    copies = [
        pltpu.make_async_copy(far, near, sems.at[i])
        for i, (far, near) in enumerate(
            (
                (map_far, time_weight),
                (guess_far, guess),
                (weight_far, space_weight),
                (noise_far, noise),
                (start_far, start),
            )
        )
    ]
    for copy in copies:
        copy.start()
    col = lax.broadcasted_iota(jnp.int32, (8, SIDE, C), 1)
    padded[0] = jnp.zeros((SIDE, 3 * C), BF16)
    padded[SIDE + 1] = jnp.zeros((SIDE, 3 * C), BF16)
    copies[0].wait()
    lane = lax.broadcasted_iota(jnp.int32, (8, C), 1)
    frequency = jnp.exp((lane % HEAD_DIM).astype(F32) * (-math.log(10000.0) / HEAD_DIM))
    angles = step[0].astype(F32) * frequency
    shifted = jnp.dot(
        jnp.where(lane < HEAD_DIM, jnp.cos(angles), jnp.sin(angles)), time_weight[...],
        precision=lax.Precision.HIGHEST, preferred_element_type=F32,
    )[0:1]
    scaling, offset = 1.0 + shifted[:, :C], shifted[:, C:]
    gain = gain_s[...]
    for i, row in enumerate((scaling, offset, gain, gain_a[...])):
        params[pl.ds(i * 16, 16), :] = jnp.broadcast_to(row, (16, C))
    copies[1].wait()
    for block in range(4):
        rows = pl.ds(block * 8, 8)
        state = guess[rows]
        normed = unit(state, gain) * scaling + offset
        left = jnp.where(col == 0, 0.0, pltpu.roll(normed, 1, 1))
        right = jnp.where(col == SIDE - 1, 0.0, pltpu.roll(normed, SIDE - 1, 1))
        at = pl.ds(block * 8 + 1, 8)
        padded[at, :, 0:C] = left.astype(BF16)
        padded[at, :, C : 2 * C] = normed.astype(BF16)
        padded[at, :, 2 * C : 3 * C] = right.astype(BF16)
    for copy in copies[2:]:
        copy.wait()
    total = None
    for shift in range(3):
        part = dot(
            padded[shift : shift + SIDE].reshape(CELLS, 3 * C),
            space_weight[shift * 3 * C : (shift + 1) * 3 * C, :],
        )
        total = part if total is None else total + part
    mixed[...] = total
    time_value, coefficient = times(step)
    scale = time_value * coefficient
    last = lax.axis_index("tm_0") * lax.axis_size("tm_1") + lax.axis_index("tm_1") == STEPS - 1
    for block in range(8):
        rows = pl.ds(block * 128, 128)
        band = pl.ds(block * 4, 4)
        conv = mixed[rows, :]
        here = guess[band].reshape(128, C) + conv * jax.nn.sigmoid(conv)
        begun = start[band].reshape(128, C)
        begun_high = begun.astype(BF16).astype(F32)
        mixed[rows, :] = jnp.where(last, begun - begun_high, here)
        drawn[rows, :] = jnp.where(last, begun_high, noise[band].reshape(128, C) * scale)
    for block in range(8):
        half = CELLS // 16
        for slot, source in enumerate((mixed, mixed, drawn, drawn)):
            packed[pl.ds(block * 256 + slot, half, 4), :] = source[pl.ds(block * 128 + slot % 2, half, 2), :]
        rows = pl.ds(block * 256, 256)
        out[rows, :] = packed[rows, :].astype(BF16)


def owner_kernel(
    all_steps, received, params, attention_weight, output_weight, states, rest_before, own_share,
    wide, drifts, *room,
):
    wide[...] = received[...].astype(F32)

    def load(block):
        return wide[pl.ds(block % 4 * 512 + block // 4, 128, 4), :]

    def emit(block, found):
        drifts[pl.ds(block * 128, 128), :] = load(block) + found

    attend(load, emit, params[48:49, :], attention_weight, output_weight, *room)
    coefficients = [(0.5 + all_steps[step].astype(F32) / 1000.0) / math.sqrt(STEPS) for step in range(STEPS)]
    here = lax.axis_index("tm_0") * lax.axis_size("tm_1") + lax.axis_index("tm_1")
    shares, own = [], jnp.float32(0.0)
    for step, coefficient in enumerate(coefficients):
        shares.append(coefficient if step == 0 else shares[-1] + coefficient)
        own = jnp.where(here == step, shares[-1], own)
    own_share[...] = jnp.full((1, C), own, F32)
    for cell in range(2):
        tail = (STEPS - 1) * FRAMES * 4 + cell
        begun = wide[pl.ds(tail + 2, FRAMES, 4), :] + wide[pl.ds(tail, FRAMES, 4), :]
        state, noises = begun, jnp.zeros((FRAMES, C), F32)
        for step in range(STEPS):
            rows = pl.ds(step * 32 + cell * FRAMES, FRAMES)
            states[rows, :] = state.astype(BF16)
            rest_before[rows, :] = noises - shares[step] * begun
            if step < STEPS - 1:
                drawn = wide[pl.ds(step * FRAMES * 4 + 2 + cell, FRAMES, 4), :]
                drift = drifts[pl.ds(cell * 512 + step * FRAMES, FRAMES), :]
                state = state + (coefficients[step] * drift + drawn)
                noises = noises + drawn


def norm_kernel(state, params, inner, outer):
    odd = lax.axis_index("frame") % 2 == 1
    for block in range(4):
        rows = pl.ds(block * 8, 8)
        pair = [
            unit(state[rows, cell].astype(F32), params[32:33, :]) * params[0:1, :] + params[16:17, :]
            for cell in range(2)
        ]
        inner[rows] = jnp.where(odd, pair[0], pair[1]).astype(BF16)
        outer[rows] = jnp.where(odd, pair[1], pair[0]).astype(BF16)


def second_kernel(
    step, state, inner, outer, from_core, from_chip, space_weight, params, attention_weight, output_weight,
    out, padded, mixed, *room,
):
    odd = lax.axis_index("frame") % 2 == 1
    columns = ((from_chip, from_core), (outer, inner), (inner, outer), (from_core, from_chip))
    for col, (when_even, when_odd) in enumerate(columns):
        padded[col, 0] = jnp.zeros((FRAMES, C), BF16)
        padded[col, SIDE + 1] = jnp.zeros((FRAMES, C), BF16)

        @pl.when(odd)
        def _(col=col, piece=when_odd):
            padded[col, 1 : SIDE + 1] = piece[...]

        @pl.when(jnp.logical_not(odd))
        def _(col=col, piece=when_even):
            padded[col, 1 : SIDE + 1] = piece[...]

    for cell in range(2):
        taps = [
            padded[cell + across, down : down + SIDE].reshape(SIDE * FRAMES, C)
            for down in range(3)
            for across in range(3)
        ]
        mixed[pl.ds(cell * 512, 512), :] = dot(jnp.concatenate(taps, axis=-1), space_weight[...])
    coefficient = times(step)[1]
    for block in range(8):
        rows = pl.ds(block * 128, 128)
        found = mixed[rows, :]
        here = state[pl.ds(block % 4 * 8, 8), block // 4].reshape(128, C).astype(F32)
        mixed[rows, :] = here + found * jax.nn.sigmoid(found)

    def load(block):
        return mixed[pl.ds(block * 128, 128), :]

    def emit(block, found):
        drift = coefficient * (load(block) + found)
        out[pl.ds(block % 4 * 8, 8), block // 4] = drift.reshape(8, FRAMES, C).astype(BF16)

    attend(load, emit, params[48:49, :], attention_weight, output_weight, *room)


def sum_kernel(received, rest_before, out, turned):
    for cell in range(2):
        total = jnp.zeros((FRAMES, C), F32)
        for step in range(STEPS):
            rows = pl.ds(step * 32 + cell * FRAMES, FRAMES)
            total = total + received[rows, :].astype(F32)
            turned[pl.ds(step * 32 + cell, FRAMES, 2), :] = total + rest_before[rows, :]
    out[...] = turned[...].astype(BF16)


def call(kernel, outs, operands, scratch, flops, spaces=(), grant=16):
    specs = [*spaces, *[VMEM] * (len(operands) - len(spaces))]
    moved = sum(x.size * x.dtype.itemsize for x in (*operands, *outs))
    return pl.pallas_call(
        kernel,
        out_shape=outs,
        in_specs=specs,
        out_specs=[VMEM] * len(outs),
        scratch_shapes=scratch,
        compiler_params=pltpu.CompilerParams(vmem_limit_bytes=grant << 20),
        cost_estimate=pl.CostEstimate(flops=flops, bytes_accessed=moved, transcendentals=0),
    )(*operands)


def attention_room():
    return [
        pltpu.VMEM((CELLS, C), BF16),
        pltpu.VMEM((CELLS, 2 * C), BF16),
        pltpu.VMEM((C, CELLS), BF16),
        pltpu.VMEM((C, CELLS), BF16),
    ]


def struct(shape, dtype):
    return jax.ShapeDtypeStruct(shape, dtype)


def exchange(array, axes):
    return lax.all_to_all(array, axes, 0, 0, tiled=True)


def shards(
    start_state,
    initial_guess,
    noise_draws,
    timesteps,
    gain_space,
    gain_attention,
    time_weight,
    space_weight,
    attention_weight,
    output_weight,
):
    guess, noise, start = initial_guess[0, 0], noise_draws[0, 0], start_state[0]
    time_value = timesteps[0].astype(F32) / 1000.0
    own_scale = time_value * (0.5 + time_value) / math.sqrt(STEPS)
    gain_space, own_scale = lax.optimization_barrier((gain_space, own_scale))
    sent, params = call(
        first_kernel,
        [struct((2 * CELLS, C), BF16), struct((64, C), F32)],
        (
            timesteps, guess, noise, start, space_weight, time_weight,
            gain_space[None, :], gain_attention[None, :],
        ),
        [
            pltpu.VMEM((SIDE, SIDE, C), F32),
            pltpu.VMEM((SIDE, SIDE, C), F32),
            pltpu.VMEM((SIDE, SIDE, C), F32),
            pltpu.VMEM((9 * C, C), BF16),
            pltpu.VMEM((C, 2 * C), F32),
            pltpu.VMEM((SIDE + 2, SIDE, 3 * C), BF16),
            pltpu.VMEM((CELLS, C), F32),
            pltpu.VMEM((CELLS, C), F32),
            pltpu.VMEM((2 * CELLS, C), F32),
            pltpu.SemaphoreType.DMA((5,)),
        ],
        2 * CELLS * 9 * C * C,
        (SMEM, FAR, FAR, FAR, FAR, FAR),
        62,
    )
    received = exchange(sent.reshape(512, 4, C), ALL).reshape(2 * CELLS, C)
    all_steps = lax.all_gather(timesteps, TM, tiled=True)
    states, rest_before, own_share = call(
        owner_kernel,
        [struct((CELLS, C), BF16), struct((CELLS, C), F32), struct((1, C), F32)],
        (all_steps, received, params, attention_weight, output_weight),
        [pltpu.VMEM((2 * CELLS, C), F32), pltpu.VMEM((CELLS, C), F32), *attention_room()],
        2 * CELLS * 8 * C * C,
        (SMEM,),
    )
    state = exchange(states.reshape(32, 32, C), TM).reshape(SIDE, 2, FRAMES, C)
    inner, outer = call(
        norm_kernel,
        [struct((SIDE, FRAMES, C), BF16)] * 2,
        (state, params),
        [],
        10 * CELLS * C,
    )
    count = lax.axis_size("frame")
    chips = [(k + i, k + 1 - i) for k in range(1, count - 1, 2) for i in range(2)]
    cores = [(k, k ^ 1) for k in range(count)]
    from_chip = lax.ppermute(outer, "frame", chips)
    from_core = lax.ppermute(inner, "frame", cores)
    (drifts,) = call(
        second_kernel,
        [struct((SIDE, 2, FRAMES, C), BF16)],
        (
            timesteps, state, inner, outer, from_core, from_chip, space_weight, params,
            attention_weight, output_weight,
        ),
        [pltpu.VMEM((4, SIDE + 2, FRAMES, C), BF16), pltpu.VMEM((CELLS, C), F32), *attention_room()],
        2 * CELLS * 17 * C * C,
        (SMEM,),
    )
    drifts = exchange(drifts.reshape(32, 32, C), TM).reshape(CELLS, C)
    (rest,) = call(
        sum_kernel,
        [struct((CELLS, C), BF16)],
        (drifts, rest_before),
        [pltpu.VMEM((CELLS, C), F32)],
        2 * CELLS * C,
    )
    rest = exchange(rest.reshape(512, 2, C), ALL).reshape(SIDE, SIDE, C).astype(F32)
    advanced = start + ((own_share * start + rest) + own_scale * noise)
    return advanced[None, None]


def solution(mesh):
    finer = Mesh(mesh.devices.reshape(4, 8, mesh.shape["frame"]), ALL)
    placed = (
        P("frame", None, None, None),
        P(TM, "frame", None, None, None),
        P(TM, "frame", None, None, None),
        P(TM),
        P(),
        P(),
        P(),
        P(),
        P(),
        P(),
    )
    return jax.shard_map(
        shards,
        mesh=finer,
        in_specs=placed,
        out_specs=P(TM, "frame", None, None, None),
        check_vma=False,
    )
```

```python
import math

import jax
import jax.numpy as jnp
from jax import lax
from jax.experimental import pallas as pl
from jax.experimental.pallas import tpu as pltpu
from jax.sharding import Mesh
from jax.sharding import PartitionSpec as P

C = 128
HEAD_DIM = 64
FRAMES = 16
STEPS = 32
SIDE = 32
CELLS = SIDE * SIDE
TM = ("tm_0", "tm_1")
ALL = ("tm_0", "tm_1", "frame")
F32 = jnp.float32
BF16 = jnp.bfloat16
VMEM = pl.BlockSpec(memory_space=pltpu.VMEM)
SMEM = pl.BlockSpec(memory_space=pltpu.SMEM)
FAR = pl.BlockSpec(memory_space=pltpu.HBM)


def dot(left, right):
    return jnp.dot(left, right, preferred_element_type=F32)


def unit(field, gain):
    return field * lax.rsqrt(jnp.mean(field * field, axis=-1, keepdims=True) + 1e-06) * gain


def attend(load, emit, gain, attention_weight, output_weight, normed, query_key, values_t, attended_t):
    row = lax.broadcasted_iota(jnp.int32, (128, 128), 0)
    lane = lax.broadcasted_iota(jnp.int32, (128, 128), 1)
    first_head = lane < HEAD_DIM
    same_cell = row // FRAMES == lane // FRAMES
    zero = jnp.zeros((), BF16)
    for block in range(8):
        normed[pl.ds(block * 128, 128), :] = unit(load(block), gain).astype(BF16)
    query_key[...] = dot(normed[...], attention_weight[:, 0 : 2 * C]).astype(BF16)
    values_t[...] = lax.dot_general(
        attention_weight[:, 2 * C :].T, normed[...], (((1,), (1,)), ((), ())), preferred_element_type=F32
    ).astype(BF16)
    for block in range(8):
        rows = pl.ds(block * 128, 128)
        keys = query_key[rows, C : 2 * C]
        keys = jnp.concatenate(
            [jnp.where(first_head, keys, zero), jnp.where(first_head, zero, keys)], axis=0
        )
        scores_t = lax.dot_general(
            keys, query_key[rows, 0:C], (((1,), (1,)), ((), ())), preferred_element_type=F32
        )
        parts = []
        for head in range(2):
            kept = jnp.where(same_cell, scores_t[head * 128 : (head + 1) * 128], 0.0)
            scores = jnp.sum(kept.reshape(8, FRAMES, 128), axis=0) * (1.0 / math.sqrt(HEAD_DIM))
            grown = jnp.exp(scores - jnp.max(scores, axis=0, keepdims=True))
            weights = grown * (1.0 / jnp.sum(grown, axis=0, keepdims=True))
            spread = jnp.where(same_cell, jnp.concatenate([weights] * 8, axis=0), 0.0)
            held = values_t[head * HEAD_DIM : (head + 1) * HEAD_DIM, rows]
            parts.append(dot(held, spread.astype(BF16)))
        attended_t[:, rows] = jnp.concatenate(parts, axis=0).astype(BF16)
    for block in range(8):
        emit(
            block,
            lax.dot_general(
                attended_t[:, pl.ds(block * 128, 128)],
                output_weight[...],
                (((0,), (0,)), ((), ())),
                preferred_element_type=F32,
            ),
        )


def times(step):
    value = step[0].astype(F32) / 1000.0
    return value, (0.5 + value) / math.sqrt(STEPS)


def first_kernel(
    step, guess_far, noise_far, start_far, weight_far, map_far, gain_s, gain_a, out, params, steps_row,
    guess, noise, start, space_weight, time_weight, padded, mixed, drawn, packed, sems,
):
    copies = [
        pltpu.make_async_copy(far, near, sems.at[i])
        for i, (far, near) in enumerate(
            (
                (map_far, time_weight),
                *((guess_far.at[pl.ds(i * 8, 8)], guess.at[pl.ds(i * 8, 8)]) for i in range(4)),
                (weight_far, space_weight),
                (noise_far, noise),
                (start_far, start),
            )
        )
    ]
    for copy in copies:
        copy.start()
    col = lax.broadcasted_iota(jnp.int32, (8, SIDE, C), 1)
    padded[0] = jnp.zeros((SIDE, 3 * C), BF16)
    padded[SIDE + 1] = jnp.zeros((SIDE, 3 * C), BF16)
    copies[0].wait()
    lane = lax.broadcasted_iota(jnp.int32, (8, C), 1)
    frequency = jnp.exp((lane % HEAD_DIM).astype(F32) * (-math.log(10000.0) / HEAD_DIM))
    angles = step[0].astype(F32) * frequency
    shifted = jnp.dot(
        jnp.where(lane < HEAD_DIM, jnp.cos(angles), jnp.sin(angles)), time_weight[...],
        precision=lax.Precision.HIGHEST, preferred_element_type=F32,
    )[0:1]
    scaling, offset = 1.0 + shifted[:, :C], shifted[:, C:]
    gain = gain_s[...]
    for i, row in enumerate((scaling, offset, gain, gain_a[...])):
        params[pl.ds(i * 16, 16), :] = jnp.broadcast_to(row, (16, C))
    for block in range(4):
        copies[1 + block].wait()
        rows = pl.ds(block * 8, 8)
        state = guess[rows]
        normed = unit(state, gain) * scaling + offset
        left = jnp.where(col == 0, 0.0, pltpu.roll(normed, 1, 1))
        right = jnp.where(col == SIDE - 1, 0.0, pltpu.roll(normed, SIDE - 1, 1))
        at = pl.ds(block * 8 + 1, 8)
        padded[at, :, 0:C] = left.astype(BF16)
        padded[at, :, C : 2 * C] = normed.astype(BF16)
        padded[at, :, 2 * C : 3 * C] = right.astype(BF16)
    for copy in copies[5:]:
        copy.wait()
    total = None
    for shift in range(3):
        part = dot(
            padded[shift : shift + SIDE].reshape(CELLS, 3 * C),
            space_weight[shift * 3 * C : (shift + 1) * 3 * C, :],
        )
        total = part if total is None else total + part
    mixed[...] = total
    time_value, coefficient = times(step)
    scale = time_value * coefficient
    place = lax.axis_index("tm_0") * lax.axis_size("tm_1") + lax.axis_index("tm_1")
    last = place == STEPS - 1
    steps_row[...] = jnp.where(lax.broadcasted_iota(jnp.int32, (1, C), 1) == place, step[0], 0)
    for block in range(8):
        rows = pl.ds(block * 128, 128)
        band = pl.ds(block * 4, 4)
        conv = mixed[rows, :]
        here = guess[band].reshape(128, C) + conv * jax.nn.sigmoid(conv)
        begun = start[band].reshape(128, C)
        begun_high = begun.astype(BF16).astype(F32)
        mixed[rows, :] = jnp.where(last, begun - begun_high, here)
        drawn[rows, :] = jnp.where(last, begun_high, noise[band].reshape(128, C) * scale)
    for block in range(8):
        half = CELLS // 16
        for slot, source in enumerate((mixed, mixed, drawn, drawn)):
            packed[pl.ds(block * 256 + slot, half, 4), :] = source[pl.ds(block * 128 + slot % 2, half, 2), :]
        rows = pl.ds(block * 256, 256)
        out[rows, :] = packed[rows, :].astype(BF16)


def owner_kernel(
    all_steps, received, params, attention_weight, output_weight, states, rest_before, own_share,
    wide, drifts, *room,
):
    wide[...] = received[...].astype(F32)

    def load(block):
        return wide[pl.ds(block % 4 * 512 + block // 4, 128, 4), :]

    def emit(block, found):
        drifts[pl.ds(block * 128, 128), :] = load(block) + found

    attend(load, emit, params[48:49, :], attention_weight, output_weight, *room)
    coefficients = [(0.5 + all_steps[0, step].astype(F32) / 1000.0) / math.sqrt(STEPS) for step in range(STEPS)]
    here = lax.axis_index("tm_0") * lax.axis_size("tm_1") + lax.axis_index("tm_1")
    shares, own = [], jnp.float32(0.0)
    for step, coefficient in enumerate(coefficients):
        shares.append(coefficient if step == 0 else shares[-1] + coefficient)
        own = jnp.where(here == step, shares[-1], own)
    own_share[...] = jnp.full((1, C), own, F32)
    for cell in range(2):
        tail = (STEPS - 1) * FRAMES * 4 + cell
        begun = wide[pl.ds(tail + 2, FRAMES, 4), :] + wide[pl.ds(tail, FRAMES, 4), :]
        state, noises = begun, jnp.zeros((FRAMES, C), F32)
        for step in range(STEPS):
            rows = pl.ds(step * 32 + cell * FRAMES, FRAMES)
            states[rows, :] = state.astype(BF16)
            rest_before[rows, :] = noises - shares[step] * begun
            if step < STEPS - 1:
                drawn = wide[pl.ds(step * FRAMES * 4 + 2 + cell, FRAMES, 4), :]
                drift = drifts[pl.ds(cell * 512 + step * FRAMES, FRAMES), :]
                state = state + (coefficients[step] * drift + drawn)
                noises = noises + drawn


def norm_kernel(state, params, inner, outer):
    odd = lax.axis_index("frame") % 2 == 1
    for block in range(4):
        rows = pl.ds(block * 8, 8)
        pair = [
            unit(state[rows, cell].astype(F32), params[32:33, :]) * params[0:1, :] + params[16:17, :]
            for cell in range(2)
        ]
        inner[rows] = jnp.where(odd, pair[0], pair[1]).astype(BF16)
        outer[rows] = jnp.where(odd, pair[1], pair[0]).astype(BF16)


def second_kernel(
    step, state, inner, outer, from_core, from_chip, space_weight, params, attention_weight, output_weight,
    out, padded, mixed, *room,
):
    odd = lax.axis_index("frame") % 2 == 1
    columns = ((from_chip, from_core), (outer, inner), (inner, outer), (from_core, from_chip))
    for col, (when_even, when_odd) in enumerate(columns):
        padded[col, 0] = jnp.zeros((FRAMES, C), BF16)
        padded[col, SIDE + 1] = jnp.zeros((FRAMES, C), BF16)

        @pl.when(odd)
        def _(col=col, piece=when_odd):
            padded[col, 1 : SIDE + 1] = piece[...]

        @pl.when(jnp.logical_not(odd))
        def _(col=col, piece=when_even):
            padded[col, 1 : SIDE + 1] = piece[...]

    for cell in range(2):
        taps = [
            padded[cell + across, down : down + SIDE].reshape(SIDE * FRAMES, C)
            for down in range(3)
            for across in range(3)
        ]
        mixed[pl.ds(cell * 512, 512), :] = dot(jnp.concatenate(taps, axis=-1), space_weight[...])
    coefficient = times(step)[1]
    for block in range(8):
        rows = pl.ds(block * 128, 128)
        found = mixed[rows, :]
        here = state[pl.ds(block % 4 * 8, 8), block // 4].reshape(128, C).astype(F32)
        mixed[rows, :] = here + found * jax.nn.sigmoid(found)

    def load(block):
        return mixed[pl.ds(block * 128, 128), :]

    def emit(block, found):
        drift = coefficient * (load(block) + found)
        out[pl.ds(block % 4 * 8, 8), block // 4] = drift.reshape(8, FRAMES, C).astype(BF16)

    attend(load, emit, params[48:49, :], attention_weight, output_weight, *room)


def sum_kernel(received, rest_before, out, turned):
    for cell in range(2):
        total = jnp.zeros((FRAMES, C), F32)
        for step in range(STEPS):
            rows = pl.ds(step * 32 + cell * FRAMES, FRAMES)
            total = total + received[rows, :].astype(F32)
            turned[pl.ds(step * 32 + cell, FRAMES, 2), :] = total + rest_before[rows, :]
    out[...] = turned[...].astype(BF16)


def call(kernel, outs, operands, scratch, flops, spaces=(), grant=16):
    specs = [*spaces, *[VMEM] * (len(operands) - len(spaces))]
    moved = sum(x.size * x.dtype.itemsize for x in (*operands, *outs))
    return pl.pallas_call(
        kernel,
        out_shape=outs,
        in_specs=specs,
        out_specs=[VMEM] * len(outs),
        scratch_shapes=scratch,
        compiler_params=pltpu.CompilerParams(vmem_limit_bytes=grant << 20),
        cost_estimate=pl.CostEstimate(flops=flops, bytes_accessed=moved, transcendentals=0),
    )(*operands)


def attention_room():
    return [
        pltpu.VMEM((CELLS, C), BF16),
        pltpu.VMEM((CELLS, 2 * C), BF16),
        pltpu.VMEM((C, CELLS), BF16),
        pltpu.VMEM((C, CELLS), BF16),
    ]


def struct(shape, dtype):
    return jax.ShapeDtypeStruct(shape, dtype)


def exchange(array, axes):
    return lax.all_to_all(array, axes, 0, 0, tiled=True)


def shards(
    start_state,
    initial_guess,
    noise_draws,
    timesteps,
    gain_space,
    gain_attention,
    time_weight,
    space_weight,
    attention_weight,
    output_weight,
):
    guess, noise, start = initial_guess[0, 0], noise_draws[0, 0], start_state[0]
    time_value = timesteps[0].astype(F32) / 1000.0
    own_scale = time_value * (0.5 + time_value) / math.sqrt(STEPS)
    gain_space, own_scale = lax.optimization_barrier((gain_space, own_scale))
    sent, params, steps_row = call(
        first_kernel,
        [struct((2 * CELLS, C), BF16), struct((64, C), F32), struct((1, C), jnp.int32)],
        (
            timesteps, guess, noise, start, space_weight, time_weight,
            gain_space[None, :], gain_attention[None, :],
        ),
        [
            pltpu.VMEM((SIDE, SIDE, C), F32),
            pltpu.VMEM((SIDE, SIDE, C), F32),
            pltpu.VMEM((SIDE, SIDE, C), F32),
            pltpu.VMEM((9 * C, C), BF16),
            pltpu.VMEM((C, 2 * C), F32),
            pltpu.VMEM((SIDE + 2, SIDE, 3 * C), BF16),
            pltpu.VMEM((CELLS, C), F32),
            pltpu.VMEM((CELLS, C), F32),
            pltpu.VMEM((2 * CELLS, C), F32),
            pltpu.SemaphoreType.DMA((8,)),
        ],
        2 * CELLS * 9 * C * C,
        (SMEM, FAR, FAR, FAR, FAR, FAR),
        62,
    )
    received = exchange(sent.reshape(512, 4, C), ALL).reshape(2 * CELLS, C)
    all_steps = lax.psum(steps_row, TM)
    states, rest_before, own_share = call(
        owner_kernel,
        [struct((CELLS, C), BF16), struct((CELLS, C), F32), struct((1, C), F32)],
        (all_steps, received, params, attention_weight, output_weight),
        [pltpu.VMEM((2 * CELLS, C), F32), pltpu.VMEM((CELLS, C), F32), *attention_room()],
        2 * CELLS * 8 * C * C,
        (SMEM,),
    )
    state = exchange(states.reshape(32, 32, C), TM).reshape(SIDE, 2, FRAMES, C)
    inner, outer = call(
        norm_kernel,
        [struct((SIDE, FRAMES, C), BF16)] * 2,
        (state, params),
        [],
        10 * CELLS * C,
    )
    count = lax.axis_size("frame")
    chips = [(k + i, k + 1 - i) for k in range(1, count - 1, 2) for i in range(2)]
    cores = [(k, k ^ 1) for k in range(count)]
    from_core = lax.ppermute(inner, "frame", cores)
    from_chip = lax.ppermute(outer, "frame", chips)
    (drifts,) = call(
        second_kernel,
        [struct((SIDE, 2, FRAMES, C), BF16)],
        (
            timesteps, state, inner, outer, from_core, from_chip, space_weight, params,
            attention_weight, output_weight,
        ),
        [pltpu.VMEM((4, SIDE + 2, FRAMES, C), BF16), pltpu.VMEM((CELLS, C), F32), *attention_room()],
        2 * CELLS * 17 * C * C,
        (SMEM,),
    )
    drifts = exchange(drifts.reshape(32, 32, C), TM).reshape(CELLS, C)
    (rest,) = call(
        sum_kernel,
        [struct((CELLS, C), BF16)],
        (drifts, rest_before),
        [pltpu.VMEM((CELLS, C), F32)],
        2 * CELLS * C,
    )
    rest = exchange(rest.reshape(512, 2, C), ALL).reshape(SIDE, SIDE, C).astype(F32)
    advanced = start + ((own_share * start + rest) + own_scale * noise)
    return advanced[None, None]


def solution(mesh):
    finer = Mesh(mesh.devices.reshape(4, 8, mesh.shape["frame"]), ALL)
    placed = (
        P("frame", None, None, None),
        P(TM, "frame", None, None, None),
        P(TM, "frame", None, None, None),
        P(TM),
        P(),
        P(),
        P(),
        P(),
        P(),
        P(),
    )
    return jax.shard_map(
        shards,
        mesh=finer,
        in_specs=placed,
        out_specs=P(TM, "frame", None, None, None),
        check_vma=False,
    )
```
